256 devices in a mesh: seq: 16 (over y, x), exp: 16 (over z, core).
Axes of the slice: x: 4, y: 4, z: 8, core: 2. Of those that a mesh axis runs over, the one named last changes fastest.
Arguments:
- hidden_in: bfloat16 [8192, 2048], P(('seq', 'exp')), may hold values from -6 to 6
- query_proj: bfloat16 [8192, 2048], P('seq', 'exp'), may hold values from -40 to 40
- key_proj: bfloat16 [8192, 2048], P('seq', 'exp'), may hold values from -40 to 40
- value_proj: bfloat16 [8192, 4096], P('seq', 'exp'), may hold values from -6 to 6
- gate_proj: bfloat16 [8192, 4096], P('seq', 'exp'), may hold values from -6 to 6
- log_decay: float32 [32, 8192], P('exp', 'seq'), may hold values from -0.6 to 0
- write_rate: float32 [32, 8192], P('exp', 'seq'), may hold values from 0 to 1
- head_gain: float32 [128], replicated, may hold values from 0.1 to 1.9
- out_weight: bfloat16 [4096, 2048], P('exp'), may hold values from -0.09375 to 0.09375
- post_gain: float32 [2048], replicated, may hold values from 0.1 to 1.9
- expert_ids: int32 [8192, 4], P(('seq', 'exp')), may hold values from 0 to 15, all different within a row; in each aligned block of 32 rows (0 to 31, 32 to 63, ...) at most 16 rows name the same one
- route_weight: bfloat16 [8192, 4], P(('seq', 'exp')), may hold values from 0.19921875 to 1
- gate_weight: bfloat16 [16, 2048, 512], P('exp'), may hold values from -0.125 to 0.125
- up_weight: bfloat16 [16, 2048, 512], P('exp'), may hold values from -0.125 to 0.125
- down_weight: bfloat16 [16, 512, 2048], P('exp'), may hold values from -0.25 to 0.25
Outputs:
- layer_out: bfloat16 [8192, 2048], P(('seq', 'exp'))
The draws below stay inside these ranges and needn't reach their ends.
Inputs may be any that keep to these rules, and one draw needn't show every extreme that they name: `expert_ids`: each token names 4 different experts. Within the tokens of one device (aligned blocks of 32 tokens in sequence order) no expert is named by more than 16 tokens, and in every draw some block names some expert exactly 16 times.
All inputs are finite; a program needn't handle non-finite values.
Results may differ from the reference program's by a relative error of at most 0.02.
Values may be sent and summed in bfloat16 or wider, within the bound.
A program may use at most 128 MiB of HBM per device.

```python
import math
import jax
import jax.numpy as jnp
import numpy as np
from jax import lax

D = 2048
FF = 512
DK = 128
DV = 128
KHEADS = 16
VALUE_HEAD_COUNT = 32
TOPK = 4
TOKEN_COUNT = 8192
TOK_DEV = 32
EXPERTS = 16
CAP = 16
N_SEQ = 16
N_EXP = 16


def rough_matrix(key, row_total, col_total, offset):
    piece_list = jax.random.split(key, 5)
    row_scale = jnp.exp(jax.random.uniform(piece_list[0], (row_total, 1), jnp.float32, 0.0, math.log(10.0)))
    col_scale = jnp.exp(jax.random.uniform(piece_list[1], (1, col_total), jnp.float32, -0.35, 0.35))
    shared_part = jax.random.uniform(piece_list[4], (1, col_total), jnp.float32, -1.0, 1.0) * offset
    base_draw = jax.random.normal(piece_list[2], (row_total, col_total), jnp.float32) + shared_part
    return jnp.clip(base_draw * row_scale * col_scale, -40.0, 40.0)


def head_plan(key):
    piece_list = jax.random.split(jax.random.fold_in(key, 11), 7)
    fast_share = 0.25
    middle_share = 0.35
    class_draw = jax.random.uniform(piece_list[0], (VALUE_HEAD_COUNT, 1), jnp.float32)
    fast_flag = class_draw < fast_share
    middle_flag = jnp.logical_and(jnp.logical_not(fast_flag), class_draw < fast_share + middle_share)
    fast_rate = -1.0 / jax.random.uniform(piece_list[1], (VALUE_HEAD_COUNT, 1), jnp.float32, 30.0, 50.0)
    middle_rate = -1.0 / jax.random.uniform(piece_list[6], (VALUE_HEAD_COUNT, 1), jnp.float32, 100.0, 240.0)
    slow_rate = -jax.random.uniform(piece_list[2], (VALUE_HEAD_COUNT, 1), jnp.float32, 0.03, 0.2) * math.log(10.0) / TOKEN_COUNT
    head_speed = jnp.where(fast_flag, fast_rate, jnp.where(middle_flag, middle_rate, slow_rate))
    random_perturbation = jax.random.uniform(piece_list[3], (VALUE_HEAD_COUNT, TOKEN_COUNT), jnp.float32, 0.5, 1.5)
    spike_location = jax.random.randint(piece_list[4], (VALUE_HEAD_COUNT, 2), 0, TOKEN_COUNT)
    spike_retention = jax.random.uniform(piece_list[5], (VALUE_HEAD_COUNT, 2), jnp.float32, 0.6, 0.8)
    token_position = jnp.arange(TOKEN_COUNT, dtype=jnp.int32)[None, :, None]
    spike_logarithm = jnp.sum(jnp.where(token_position == spike_location[:, None, :], jnp.log(spike_retention)[:, None, :], 0.0), axis=2)
    return (fast_flag, middle_flag, head_speed * random_perturbation + spike_logarithm)


def draw_query_proj(key, part):
    return rough_matrix(jax.random.fold_in(key, 3), TOKEN_COUNT, KHEADS * DK, 0.0).astype(jnp.bfloat16)


def draw_key_proj(key, part):
    return rough_matrix(jax.random.fold_in(key, 5), TOKEN_COUNT, KHEADS * DK, 2.5).astype(jnp.bfloat16)


def draw_log_decay(key, part):
    fast_flag, middle_flag, decay_log = head_plan(key)
    return decay_log


def draw_write_rate(key, part):
    fast_flag, middle_flag, decay_log = head_plan(key)
    piece_list = jax.random.split(jax.random.fold_in(key, 23), 3)
    fast_rate = jax.random.uniform(piece_list[0], (VALUE_HEAD_COUNT, TOKEN_COUNT), jnp.float32, 0.3, 0.9)
    middle_rate = jax.random.uniform(piece_list[2], (VALUE_HEAD_COUNT, TOKEN_COUNT), jnp.float32, 0.1, 0.3)
    slow_rate = DK / TOKEN_COUNT * jax.random.uniform(piece_list[1], (VALUE_HEAD_COUNT, TOKEN_COUNT), jnp.float32, 1.5, 3.0)
    return jnp.where(fast_flag, fast_rate, jnp.where(middle_flag, middle_rate, slow_rate))


def steps_of(stream_key, shape, cuts, low, largest):
    factor_of, own = 1.0, jax.random.fold_in(stream_key, 6)
    for axis_at, shards_of in cuts:
        draws = jnp.exp(jax.random.uniform(jax.random.fold_in(own, axis_at), (shards_of,), jnp.float32, low / len(cuts), largest / len(cuts)))
        factor_of = factor_of * jnp.repeat(draws, shape[axis_at] // shards_of).reshape([-1 if axis == axis_at else 1 for axis in range(len(shape))])
    return factor_of


def assign_block(own_key, own, number, rows, count, top, limit, lean):
    ranking = jax.random.permutation(own_key, count)
    heavy_load, ordinary = shares(count, rows * top, limit, lean, True), shares(count, rows * top, limit, lean, False)
    places = jnp.arange(count)

    def named(tallies, turn):
        used = int((tallies > 0).sum())
        fixed = max(1, used // 4)
        passed = fixed + (places - fixed + turn * (used - fixed)) % max(1, count - fixed)
        return jnp.zeros((count,), jnp.int32).at[ranking[jnp.where(places < fixed, places, passed)]].set(jnp.asarray(tallies, jnp.int32))

    tallies = jnp.where(number % 4 == 0, named(heavy_load, number // 4), named(ordinary, number - number // 4 - 1))
    mixed = jax.random.permutation(jax.random.fold_in(own, 3), count)
    giver, taker = mixed[0:count // 2 * 2:2], mixed[1:count // 2 * 2:2]
    margin = jnp.minimum(tallies[giver] - 1, limit - tallies[taker]) // 2
    margin = jnp.where((giver == ranking[0]) | (taker == ranking[0]) | (tallies[taker] == 0), 0, jnp.maximum(margin, 0))
    passed = jax.random.randint(jax.random.fold_in(own, 4), (count // 2,), 0, 1 << 20) % (margin + 1)
    tallies = tallies.at[giver].add(-passed).at[taker].add(passed)
    labels = jnp.searchsorted(jnp.cumsum(tallies), jnp.arange(rows * top), side="right").astype(jnp.int32)
    listing = labels.reshape(top, rows).T
    listing = listing[jax.random.permutation(jax.random.fold_in(own, 1), rows)]
    turn = jax.random.randint(jax.random.fold_in(own, 2), (rows, 1), 0, top)
    return jnp.take_along_axis(listing, (jnp.arange(top)[None, :] + turn) % top, axis=1)


def shares(number_of, total, bound, slope, full):
    weights = [(1 << 20) // math.isqrt(grade ** slope) + 1 for grade in range(1, number_of + 1)]
    largest = bound if full else min(bound, max(-(-total // number_of), total * weights[0] // sum(weights)))
    least = 1 if total - largest >= number_of - 1 else 0
    given, surplus = [largest] + [least] * (number_of - 1), total - largest - least * (number_of - 1)
    while surplus > 0:
        movable = [i for i in range(1, number_of) if given[i] < largest] or [i for i in range(1, number_of) if given[i] < bound]
        whole, remaining = sum([weights[i] for i in movable]), surplus
        for i in movable:
            addition = min(bound - given[i], max(1, remaining * weights[i] // whole), surplus)
            given[i] = given[i] + addition
            surplus = surplus - addition
    return np.array(given)


def centred(stream_key, dims, width, most, shards=(), held_as=jnp.bfloat16):
    entries = jax.random.normal(stream_key, dims, jnp.float32) * width
    if len(shards) > 0:
        entries = steps_of(stream_key, dims, shards, -0.22, 0.18) * entries
    return jnp.clip(entries, min=-most, max=most).astype(held_as)


def setup_inputs(seed: int = 0) -> dict:
    seeds = jax.random.split(jax.random.key(seed), 16)
    hidden_in = centred(seeds[0], (TOKEN_COUNT, D), 1.0, 6.0, ((0, 256),))
    query_proj = draw_query_proj(jax.random.fold_in(seeds[15], 71), 0)
    key_proj = draw_key_proj(jax.random.fold_in(seeds[15], 71), 0)
    value_proj = centred(seeds[3], (TOKEN_COUNT, VALUE_HEAD_COUNT * DV), 1.0, 6.0, ((0, 16), (1, 16)))
    gate_proj = centred(seeds[4], (TOKEN_COUNT, VALUE_HEAD_COUNT * DV), 1.0, 6.0, ((0, 16), (1, 16)))
    log_decay = draw_log_decay(jax.random.fold_in(seeds[15], 71), 0)
    write_rate = draw_write_rate(jax.random.fold_in(seeds[15], 71), 0)
    head_gain = jnp.clip(1.0 + 0.18 * jax.random.normal(seeds[7], (DV,), jnp.float32), 0.1, 1.9)
    out_weight = centred(seeds[8], (VALUE_HEAD_COUNT * DV, D), (VALUE_HEAD_COUNT * DV) ** -0.5, 0.09375, ((0, 16),))
    post_gain = jnp.clip(1.0 + 0.18 * jax.random.normal(seeds[9], (D,), jnp.float32), 0.1, 1.9)
    expert_ids_keys = jax.random.split(jax.random.fold_in(seeds[10], 1), TOKEN_COUNT // TOK_DEV)
    expert_ids_turns = jax.random.permutation(jax.random.fold_in(seeds[10], 3), TOKEN_COUNT // TOK_DEV)
    expert_ids = jax.vmap(lambda own, number: assign_block(jax.random.fold_in(seeds[10], 2), own, number, TOK_DEV, EXPERTS, TOPK, CAP, 2))(expert_ids_keys, expert_ids_turns).reshape((TOKEN_COUNT, TOPK))
    route_weight = jnp.clip(0.19921875 + 0.80078125 * jax.random.uniform(seeds[11], (TOKEN_COUNT, TOPK), jnp.float32) ** steps_of(seeds[11], (TOKEN_COUNT, TOPK), ((0, 256),), -0.2, 0.2), 0.19921875, 1.0).astype(jnp.bfloat16)
    gate_weight = centred(seeds[12], (EXPERTS, D, FF), D ** -0.5, 0.125, ((0, 16),))
    up_weight = centred(seeds[13], (EXPERTS, D, FF), D ** -0.5, 0.125, ((0, 16),))
    down_weight = centred(seeds[14], (EXPERTS, FF, D), FF ** -0.5, 0.25, ((0, 16),))
    return dict(hidden_in=hidden_in, query_proj=query_proj, key_proj=key_proj, value_proj=value_proj, gate_proj=gate_proj, log_decay=log_decay, write_rate=write_rate, head_gain=head_gain, out_weight=out_weight, post_gain=post_gain, expert_ids=expert_ids, route_weight=route_weight, gate_weight=gate_weight, up_weight=up_weight, down_weight=down_weight)


EPS = 1e-06
HIGHEST_ACCURACY = lax.Precision.HIGHEST

def unit_rows(matrix):
    return matrix * lax.rsqrt(lax.optimization_barrier(jnp.sum(matrix * matrix, axis=-1, keepdims=True)) + EPS)

def reference(hidden_in, query_proj, key_proj, value_proj, gate_proj, log_decay, write_rate, head_gain, out_weight, post_gain, expert_ids, route_weight, gate_weight, up_weight, down_weight):
    group_size = VALUE_HEAD_COUNT // KHEADS

    def advance(carried, inputs):
        query_row, key_row, value_row, gate_row, decay_row, rate_row = inputs
        query_unit = unit_rows(query_row.astype(jnp.float32).reshape(KHEADS, DK)) * DK ** (-0.5)
        key_unit = unit_rows(key_row.astype(jnp.float32).reshape(KHEADS, DK))
        query_unit = jnp.repeat(query_unit, group_size, axis=0)
        key_unit = jnp.repeat(key_unit, group_size, axis=0)
        value_heads = value_row.astype(jnp.float32).reshape(VALUE_HEAD_COUNT, DV)
        retain = jnp.exp(decay_row)
        recalled = jnp.einsum('hvk,hk->hv', carried, key_unit, precision=HIGHEST_ACCURACY)
        carried = retain[:, None, None] * (carried - rate_row[:, None, None] * recalled[:, :, None] * key_unit[:, None, :]) + rate_row[:, None, None] * value_heads[:, :, None] * key_unit[:, None, :]
        readout = jnp.einsum('hvk,hk->hv', carried, query_unit, precision=HIGHEST_ACCURACY)
        gate_heads = gate_row.astype(jnp.float32).reshape(VALUE_HEAD_COUNT, DV)
        scaled = readout * lax.rsqrt(lax.optimization_barrier(jnp.mean(readout * readout, axis=-1, keepdims=True)) + EPS)
        mixed_row = scaled * head_gain * jax.nn.silu(gate_heads)
        return (carried, mixed_row.reshape(VALUE_HEAD_COUNT * DV).astype(jnp.bfloat16))
    initial = jnp.zeros((VALUE_HEAD_COUNT, DV, DK), jnp.float32)
    unused_state, mixed = lax.scan(advance, initial, (query_proj, key_proj, value_proj, gate_proj, log_decay.T, write_rate.T))
    residual = hidden_in.astype(jnp.float32) + jnp.dot(mixed, out_weight, preferred_element_type=jnp.float32)
    normed = (residual * lax.rsqrt(lax.optimization_barrier(jnp.mean(residual * residual, axis=-1, keepdims=True)) + EPS) * post_gain).astype(jnp.bfloat16)
    row_total = TOKEN_COUNT * TOPK
    room_rows = N_SEQ * N_EXP * CAP
    flat_ids = expert_ids.reshape(-1)
    flat_weight = route_weight.reshape(-1).astype(jnp.float32)
    owner_tok = jnp.arange(row_total, dtype=jnp.int32) // TOPK

    def add_expert(running_sum, expert):
        is_hit = flat_ids == expert
        token_position = jnp.cumsum(is_hit.astype(jnp.int32)) - 1
        target = jnp.where(is_hit, token_position, room_rows).astype(jnp.int32)
        sources = jnp.zeros((room_rows,), jnp.int32).at[target].set(owner_tok, mode='drop')
        slot_weight = jnp.zeros((room_rows,), jnp.float32).at[target].set(flat_weight, mode='drop')
        picked = normed[sources]
        gate_act = jnp.dot(picked, gate_weight[expert], preferred_element_type=jnp.float32)
        up_act = jnp.dot(picked, up_weight[expert], preferred_element_type=jnp.float32)
        hidden = (jax.nn.silu(gate_act) * up_act).astype(jnp.bfloat16)
        produced = jnp.dot(hidden, down_weight[expert], preferred_element_type=jnp.float32).astype(jnp.bfloat16)
        running_sum = running_sum.at[sources].add(produced.astype(jnp.float32) * slot_weight[:, None])
        return (running_sum, None)
    combined, unused_out = lax.scan(add_expert, residual, jnp.arange(EXPERTS, dtype=jnp.int32))
    return combined.astype(jnp.bfloat16)
```

```python
import functools

import jax
import jax.numpy as jnp
from jax import lax
from jax.experimental import pallas as pl
from jax.experimental.pallas import tpu as pltpu
from jax.sharding import PartitionSpec as P

D = 2048
FF = 512
DK = 128
DV = 128
EPS = 1e-06
CH = 128
HALF = D // 2
F32 = jnp.float32
BF16 = jnp.bfloat16
MESH = pl.DeviceIdType.MESH
NN = (((1,), (0,)), ((), ()))
NT = (((1,), (1,)), ((), ()))
TN = (((0,), (0,)), ((), ()))


def mm(a, b, dims=NN):
    return lax.dot_general(a, b, dims, preferred_element_type=F32)


def split(a):
    hi = a.astype(BF16)
    return hi, (a - hi.astype(F32)).astype(BF16)


def mm3(a, b, dims=NN):
    ah, al = a if isinstance(a, tuple) else split(a)
    bh, bl = b if isinstance(b, tuple) else split(b)
    return mm(ah, bh, dims) + (mm(ah, bl, dims) + mm(al, bh, dims))


def mm2(a, b, dims=NN):
    bh, bl = split(b)
    return mm(a, bh, dims) + mm(a, bl, dims)


def greet(axis, peers):
    barrier = pltpu.get_barrier_semaphore()
    for peer in peers:
        pl.semaphore_signal(barrier, inc=1, device_id={axis: peer}, device_id_type=MESH)
    pl.semaphore_wait(barrier, len(peers))


def send_to(src, dst, send_sem, recv_sem, axis, peer):
    return pltpu.make_async_remote_copy(
        src_ref=src,
        dst_ref=dst,
        send_sem=send_sem,
        recv_sem=recv_sem,
        device_id={axis: peer},
        device_id_type=MESH,
    )


class Gather4:
    def __init__(self, slots, me, right, left, ssem, rsem):
        before, after = lax.rem(me + 3, 4), lax.rem(me + 1, 4)
        self.own = [
            send_to(slots.at[me], slots.at[me], ssem.at[0], rsem.at[0], "seq", right),
            send_to(slots.at[me], slots.at[me], ssem.at[1], rsem.at[1], "seq", left),
        ]
        self.arrive = [
            send_to(slots.at[before], slots.at[before], ssem.at[0], rsem.at[0], "seq", right),
            send_to(slots.at[after], slots.at[after], ssem.at[1], rsem.at[1], "seq", left),
        ]
        self.onward = [
            send_to(
                slots.at[before, 0], slots.at[before, 0], ssem.at[2], rsem.at[2], "seq", right
            ),
            send_to(slots.at[after, 1], slots.at[after, 1], ssem.at[3], rsem.at[3], "seq", left),
        ]
        far = lax.rem(me + 2, 4)
        self.far = [
            send_to(slots.at[far, 0], slots.at[far, 0], ssem.at[2], rsem.at[2], "seq", right),
            send_to(slots.at[far, 1], slots.at[far, 1], ssem.at[3], rsem.at[3], "seq", left),
        ]

    def start(self):
        for copy in self.own:
            copy.start()

    def forward(self):
        for came, on in zip(self.arrive, self.onward):
            came.wait_recv()
            on.start()

    def finish(self):
        for copy in self.far:
            copy.wait_recv()

    def drain(self):
        for copy in self.own + self.onward:
            copy.wait_send()


def compose(later, earlier):
    later = later.astype(F32)
    earlier = earlier.astype(F32)
    joined = mm3(later[:, :DK], earlier)
    return joined + jnp.concatenate([jnp.zeros((DK, DK), F32), later[:, DK:]], axis=1)


def seq_kernel(
    q_ref,
    k_ref,
    v_ref,
    g_ref,
    ld_ref,
    wr_ref,
    gain_ref,
    o_ref,
    xs,
    ys,
    xsend,
    xrecv,
    ysend,
    yrecv,
):
    place = lax.axis_index("seq")
    x, y = lax.rem(place, 4), lax.div(place, 4)
    x_right, x_left = y * 4 + lax.rem(x + 1, 4), y * 4 + lax.rem(x + 3, 4)
    y_right, y_left = lax.rem(y + 1, 4) * 4 + x, lax.rem(y + 3, 4) * 4 + x
    greet("seq", (x_right, x_left, y_right, y_left))

    chunks = q_ref.shape[0] // CH
    row = lax.broadcasted_iota(jnp.int32, (CH, CH), 0)
    col = lax.broadcasted_iota(jnp.int32, (CH, CH), 1)
    eye = row == col
    causal = row >= col
    strict = row > col
    pairs = [(n, h) for n in range(chunks) for h in range(2)]

    keys, kk, qk, queries = [], [], [], []
    for n in range(chunks):
        rows = slice(n * CH, (n + 1) * CH)
        k = k_ref[rows, :].astype(F32)
        k = k * lax.rsqrt(jnp.sum(k * k, axis=-1, keepdims=True) + EPS)
        q = q_ref[rows, :].astype(F32)
        q = q * lax.rsqrt(jnp.sum(q * q, axis=-1, keepdims=True) + EPS) * DK ** (-0.5)
        ks = split(k)
        keys.append(k)
        queries.append(q)
        kk.append(mm3(ks, ks, NT))
        qk.append(mm3(split(q), ks, NT))

    decay, grow, tail, end, strict_part, rate = {}, {}, {}, {}, {}, {}
    for n, h in pairs:
        ld_row = ld_ref[h : h + 1, n * CH : (n + 1) * CH]
        ld_all = jnp.broadcast_to(ld_row, (CH, CH))
        wr_all = jnp.broadcast_to(wr_ref[h : h + 1, n * CH : (n + 1) * CH], (CH, CH))
        ld_col = jnp.sum(jnp.where(eye, ld_all, 0.0), axis=1, keepdims=True)
        cum_col = jnp.sum(jnp.where(causal, ld_all, 0.0), axis=1, keepdims=True)
        cum_row = jnp.sum(jnp.where(row <= col, ld_col, 0.0), axis=0, keepdims=True)
        rate[n, h] = jnp.sum(jnp.where(eye, wr_all, 0.0), axis=1, keepdims=True)
        total = jnp.sum(ld_row, axis=1, keepdims=True)
        decay[n, h] = jnp.where(causal, jnp.exp(jnp.where(causal, cum_col - cum_row, 0.0)), 0.0)
        grow[n, h] = jnp.exp(cum_col)
        tail[n, h] = jnp.exp(total - cum_col)
        end[n, h] = jnp.exp(total)
        strict_part[n, h] = jnp.where(strict, kk[n] * decay[n, h] * rate[n, h], 0.0)

    inverse = {}
    for p in pairs:
        low = jnp.where((row // 2 == col // 2) & strict, strict_part[p], 0.0)
        inverse[p] = jnp.where(eye, 1.0, -low)
    width = 2
    while width < CH:
        mask = (row // (2 * width) == col // (2 * width)) & (row // width > col // width)
        inner = {}
        held = {}
        for p in pairs:
            held[p] = split(inverse[p])
            inner[p] = mm3(split(jnp.where(mask, strict_part[p], 0.0)), held[p])
        for p in pairs:
            inverse[p] = inverse[p] - mm3(held[p], split(inner[p]))
        width *= 2

    step, solved = {}, {}
    for n, h in pairs:
        value = v_ref[n * CH : (n + 1) * CH, h * DV : (h + 1) * DV].astype(F32)
        sides = jnp.concatenate([keys[n] * (rate[n, h] * grow[n, h]), value * rate[n, h]], axis=1)
        solved[n, h] = split(mm3(inverse[n, h], sides))
    for n, h in pairs:
        fed = mm3(split(keys[n] * tail[n, h]), solved[n, h], TN)
        step[n, h] = jnp.concatenate(
            [jnp.where(eye, end[n, h], 0.0) - fed[:, :DK], fed[:, DK:]], axis=1
        )

    prefixes = {}
    for h in range(2):
        first = compose(step[1, h], step[0, h])
        second = compose(step[3, h], step[2, h])
        whole = compose(second, first)
        xs[x, h] = whole.astype(BF16)
        prefixes[1, h] = step[0, h]
        prefixes[2, h] = first
        prefixes[3, h] = (step[2, h], first)

    along_x = Gather4(xs, x, x_right, x_left, xsend, xrecv)
    along_x.start()

    base, mapped = {}, {}
    for n, h in pairs:
        scores = qk[n] * decay[n, h]
        seen = mm3(split(scores), solved[n, h])
        effective = queries[n] * grow[n, h] - seen[:, :DK]
        if n == 0:
            base[n, h], mapped[n, h] = seen[:, DK:], effective
        else:
            ahead = prefixes[n, h]
            if n == 3:
                ahead = compose(ahead[0], ahead[1])
            through = mm3(effective, ahead)
            base[n, h], mapped[n, h] = seen[:, DK:] + through[:, DK:], through[:, :DK]

    along_x.forward()
    along_x.finish()
    along_y = Gather4(ys, y, y_right, y_left, ysend, yrecv)
    for h in range(2):
        lower = compose(xs[1, h], xs[0, h])
        upper = compose(xs[3, h], xs[2, h])
        ys[y, h] = compose(upper, lower).astype(BF16)
    along_y.start()

    state = {}
    inside = {}
    start = jnp.where(
        lax.broadcasted_iota(jnp.int32, (DK, 2 * DK), 0)
        == lax.broadcasted_iota(jnp.int32, (DK, 2 * DK), 1),
        1.0,
        0.0,
    )
    for h in range(2):
        running = jnp.where(x > 0, xs[0, h].astype(F32), start)
        for other in range(1, 3):
            running = jnp.where(x > other, compose(xs[other, h], running), running)
        inside[h] = running
    along_y.forward()
    along_y.finish()
    for h in range(2):
        running = jnp.where(y > 0, ys[0, h, :, DK:].astype(F32), 0.0)
        for other in range(1, 3):
            after = mm2(ys[other, h, :, :DK], running) + ys[other, h, :, DK:].astype(F32)
            running = jnp.where(y > other, after, running)
        state[h] = split(mm3(inside[h][:, :DK], running) + inside[h][:, DK:])

    gain = gain_ref[...]
    for n, h in pairs:
        rows, cols = slice(n * CH, (n + 1) * CH), slice(h * DV, (h + 1) * DV)
        readout = base[n, h] + mm3(mapped[n, h], state[h])
        scaled = readout * lax.rsqrt(jnp.mean(readout * readout, axis=-1, keepdims=True) + EPS)
        gate = g_ref[rows, cols].astype(F32)
        o_ref[rows, cols] = (scaled * gain * (gate / (1.0 + jnp.exp(-gate)))).astype(BF16)

    along_x.drain()
    along_y.drain()


class RingSum:
    def __init__(self, own, pair_out, pair_in, out, came, psem, rsem, ring):
        self.own, self.pair_out, self.pair_in, self.out, self.came = own, pair_out, pair_in, out, came
        self.psem, self.rsem, self.ring = psem, rsem, ring
        self.sent, self.paired = [], set()

    def pair(self, d):
        return send_to(
            self.pair_out.at[d],
            self.pair_in.at[d],
            self.psem.at[0, d],
            self.psem.at[1, d],
            "exp",
            self.ring[2],
        )

    def offer(self, d):
        copy = self.pair(d)
        copy.start()
        self.sent.append(copy)

    def chip_sum(self, d, half):
        if d not in self.paired:
            self.pair(d).wait_recv()
            self.paired.add(d)
        cols = slice(half * HALF, (half + 1) * HALF)
        return self.own[d, :, cols] + self.pair_in[d, :, cols].astype(F32)

    def hop(self, way, step, half):
        return send_to(
            self.out.at[way, step, half],
            self.came.at[way, step, half],
            self.rsem.at[0, way, step, half],
            self.rsem.at[1, way, step, half],
            "exp",
            self.ring[way],
        )

    def run(self):
        for step in range(4):
            for turn in range(2):
                for way in range(2):
                    half = way if turn == 0 else 1 - way
                    if step == 0 and turn == 1:
                        continue
                    d = 4 - step if way == 0 else 4 + step
                    total = self.chip_sum(d, half)
                    if step >= 2 or (step == 1 and turn == 0):
                        self.hop(way, step - 1, half).wait_recv()
                        total = total + self.came[way, step - 1, half].astype(F32)
                    self.out[way, step, half] = total.astype(BF16)
                    copy = self.hop(way, step, half)
                    copy.start()
                    self.sent.append(copy)

    def result(self, half):
        total = self.chip_sum(0, half)
        for way in range(2):
            self.hop(way, 3, half).wait_recv()
            total = total + self.came[way, 3, half].astype(F32)
        return total

    def drain(self):
        for copy in self.sent:
            copy.wait_send()


def exp_kernel(
    mix_ref,
    hid_ref,
    ids_ref,
    route_ref,
    post_ref,
    ow_hbm,
    gw_hbm,
    uw_hbm,
    dw_hbm,
    o_ref,
    ow,
    gw,
    uw,
    dw,
    own,
    pair_out,
    pair_in,
    out,
    came,
    res,
    low,
    high,
    wsem,
    psem,
    rsem,
    gsem,
    bsem,
):
    place = lax.axis_index("exp")
    z, core = lax.div(place, 2), lax.rem(place, 2)
    right = lax.rem(z + 1, 8) * 2 + core
    left = lax.rem(z + 7, 8) * 2 + core
    sibling = z * 2 + (1 - core)
    ring = (right, left, sibling)
    loads = [
        pltpu.make_async_copy(src, dst, wsem.at[i])
        for i, (src, dst) in enumerate(((ow_hbm, ow), (gw_hbm, gw), (uw_hbm, uw), (dw_hbm, dw)))
    ]
    for load in loads:
        load.start()
    greet("exp", ring)
    loads[0].wait()

    first = RingSum(
        own.at[0],
        pair_out.at[0],
        pair_in.at[0],
        out.at[0],
        came.at[0],
        psem.at[0],
        rsem.at[0],
        ring,
    )
    weight = ow[...]
    for d in (4, 3, 5, 2, 6, 1, 7, 0):
        chip = lax.rem(z + d, 8)
        for mine in (False, True):
            part = core if mine else 1 - core
            rows = pl.ds(pl.multiple_of(chip * 64 + part * 32, 32), 32)
            block = mm(mix_ref[rows, :], weight)
            if mine:
                own[0, d] = block
            else:
                pair_out[0, d] = block.astype(BF16)
                first.offer(d)
    first.run()
    for half in range(2):
        cols = slice(half * HALF, (half + 1) * HALF)
        res[:, cols] = hid_ref[:, cols].astype(F32) + first.result(half)

    residual = res[...]
    normed = (
        residual
        * lax.rsqrt(jnp.mean(residual * residual, axis=-1, keepdims=True) + EPS)
        * post_ref[...]
    ).astype(BF16)
    low[0, 0, :, :HALF] = normed[:, :HALF]
    high[0, 0] = normed[:, HALF:]
    lane = lax.broadcasted_iota(jnp.int32, (32, 128), 1)
    table = jnp.zeros((32, 128), F32)
    for j in range(4):
        table = table + jnp.where(
            lane == ids_ref[:, j : j + 1], route_ref[:, j : j + 1].astype(F32), 0.0
        )
    low[0, 0, :, HALF:] = table.astype(BF16)

    halves = (low, high)
    sent = []

    def onward(way, step, half):
        src = (8 - step) % 8 if way == 0 else step
        dst = 7 - step if way == 0 else step + 1
        return send_to(
            halves[half].at[src, 0],
            halves[half].at[dst, 0],
            gsem.at[0, way, step, half],
            gsem.at[1, way, step, half],
            "exp",
            ring[way],
        )

    def across(d, half):
        return send_to(
            halves[half].at[d, 0],
            halves[half].at[d, 1],
            bsem.at[0, d, half],
            bsem.at[1, d, half],
            "exp",
            sibling,
        )

    def begin(copy):
        copy.start()
        sent.append(copy)

    second = RingSum(
        own.at[1],
        pair_out.at[1],
        pair_in.at[1],
        out.at[1],
        came.at[1],
        psem.at[1],
        rsem.at[1],
        ring,
    )

    def expert(offsets):
        for d in offsets:
            for half in range(2):
                across(d, half).wait_recv()
        cells = [(d, side) for d in offsets for side in range(2)]
        left_part = jnp.concatenate([low[d, side, :, :HALF] for d, side in cells], axis=0)
        right_part = jnp.concatenate([high[d, side] for d, side in cells], axis=0)
        gate = mm(left_part, gw[0, :HALF, :]) + mm(right_part, gw[0, HALF:, :])
        up = mm(left_part, uw[0, :HALF, :]) + mm(right_part, uw[0, HALF:, :])
        hidden = (gate / (1.0 + jnp.exp(-gate)) * up).astype(BF16)
        produced = mm(hidden, dw[0]).astype(BF16).astype(F32)
        for i, (d, side) in enumerate(cells):
            share = jnp.sum(
                jnp.where(lane == place, low[d, side, :, HALF:].astype(F32), 0.0),
                axis=1,
                keepdims=True,
            )
            block = produced[32 * i : 32 * i + 32] * share
            if side == 0:
                own[1, d] = block
            else:
                pair_out[1, d] = block.astype(BF16)
                second.offer(d)

    for way in range(2):
        for half in (way, 1 - way):
            begin(onward(way, 0, half))
    for half in range(2):
        begin(across(0, half))
    for load in loads[1:]:
        load.wait()
    expert((0,))
    for step in range(1, 4):
        for turn in range(2):
            for way in range(2):
                half = way if turn == 0 else 1 - way
                onward(way, step - 1, half).wait_recv()
                if step < 3 or turn == 0:
                    begin(onward(way, step, half))
                begin(across(8 - step if way == 0 else step, half))
        expert((8 - step, step))
    for way in range(2):
        onward(way, 3, way).wait_recv()
        begin(across(4, way))
    expert((4,))
    second.run()
    for half in range(2):
        cols = slice(half * HALF, (half + 1) * HALF)
        o_ref[:, cols] = (res[:, cols] + second.result(half)).astype(BF16)
    for copy in sent:
        copy.wait_send()
    first.drain()
    second.drain()


def in_vmem(count):
    return [pl.BlockSpec(memory_space=pltpu.VMEM)] * count


def seq_stage(q, k, v, g, ld, wr, gain):
    slots = pltpu.VMEM((4, 2, DK, 2 * DK), BF16)
    return pl.pallas_call(
        seq_kernel,
        out_shape=jax.ShapeDtypeStruct(v.shape, BF16),
        in_specs=in_vmem(7),
        out_specs=pl.BlockSpec(memory_space=pltpu.VMEM),
        scratch_shapes=[slots, slots] + [pltpu.SemaphoreType.DMA((4,))] * 4,
        compiler_params=pltpu.CompilerParams(
            collective_id=0, has_side_effects=True, vmem_limit_bytes=48 * 1024 * 1024
        ),
        name="seq_stage",
    )(q, k, v, g, ld, wr, gain)


def exp_stage(mixed, hidden, ids, route, post, ow, gw, uw, dw):
    scratch = [
        pltpu.VMEM(ow.shape, BF16),
        pltpu.VMEM(gw.shape, BF16),
        pltpu.VMEM(uw.shape, BF16),
        pltpu.VMEM(dw.shape, BF16),
        pltpu.VMEM((2, 8, 32, D), F32),
        pltpu.VMEM((2, 8, 32, D), BF16),
        pltpu.VMEM((2, 8, 32, D), BF16),
        pltpu.VMEM((2, 2, 4, 2, 32, HALF), BF16),
        pltpu.VMEM((2, 2, 4, 2, 32, HALF), BF16),
        pltpu.VMEM((32, D), F32),
        pltpu.VMEM((8, 2, 32, HALF + 128), BF16),
        pltpu.VMEM((8, 2, 32, HALF), BF16),
        pltpu.SemaphoreType.DMA((4,)),
        pltpu.SemaphoreType.DMA((2, 2, 8)),
        pltpu.SemaphoreType.DMA((2, 2, 2, 4, 2)),
        pltpu.SemaphoreType.DMA((2, 2, 4, 2)),
        pltpu.SemaphoreType.DMA((2, 8, 2)),
    ]
    return pl.pallas_call(
        exp_kernel,
        out_shape=jax.ShapeDtypeStruct(hidden.shape, BF16),
        in_specs=in_vmem(5) + [pl.BlockSpec(memory_space=pl.ANY)] * 4,
        out_specs=pl.BlockSpec(memory_space=pltpu.VMEM),
        scratch_shapes=scratch,
        compiler_params=pltpu.CompilerParams(
            collective_id=1, has_side_effects=True, vmem_limit_bytes=56 * 1024 * 1024
        ),
        name="exp_stage",
    )(mixed, hidden, ids, route, post, ow, gw, uw, dw)


def per_device(
    hidden_in,
    query_proj,
    key_proj,
    value_proj,
    gate_proj,
    log_decay,
    write_rate,
    head_gain,
    out_weight,
    post_gain,
    expert_ids,
    route_weight,
    gate_weight,
    up_weight,
    down_weight,
):
    mixed = seq_stage(
        query_proj,
        key_proj,
        value_proj,
        gate_proj,
        log_decay,
        write_rate,
        head_gain.reshape(1, DV),
    )
    return exp_stage(
        mixed,
        hidden_in,
        expert_ids,
        route_weight,
        post_gain.reshape(1, D),
        out_weight,
        gate_weight,
        up_weight,
        down_weight,
    )


def solution(mesh):
    in_specs = (
        P(("seq", "exp"), None),
        P("seq", "exp"),
        P("seq", "exp"),
        P("seq", "exp"),
        P("seq", "exp"),
        P("exp", "seq"),
        P("exp", "seq"),
        P(),
        P("exp", None),
        P(),
        P(("seq", "exp"), None),
        P(("seq", "exp"), None),
        P("exp", None, None),
        P("exp", None, None),
        P("exp", None, None),
    )
    out_specs = P(("seq", "exp"), None)
    return jax.shard_map(
        per_device, mesh=mesh, in_specs=in_specs, out_specs=out_specs, check_vma=False
    )
```

```python
import functools

import jax
import jax.numpy as jnp
from jax import lax
from jax.experimental import pallas as pl
from jax.experimental.pallas import tpu as pltpu
from jax.sharding import PartitionSpec as P

D = 2048
FF = 512
DK = 128
DV = 128
EPS = 1e-06
CH = 128
HALF = D // 2
F32 = jnp.float32
BF16 = jnp.bfloat16
MESH = pl.DeviceIdType.MESH
NN = (((1,), (0,)), ((), ()))
NT = (((1,), (1,)), ((), ()))
TN = (((0,), (0,)), ((), ()))


def mm(a, b, dims=NN):
    return lax.dot_general(a, b, dims, preferred_element_type=F32)


def split(a):
    hi = a.astype(BF16)
    return hi, (a - hi.astype(F32)).astype(BF16)


def mm3(a, b, dims=NN):
    ah, al = a if isinstance(a, tuple) else split(a)
    bh, bl = b if isinstance(b, tuple) else split(b)
    return mm(ah, bh, dims) + (mm(ah, bl, dims) + mm(al, bh, dims))


def mm2(a, b, dims=NN):
    bh, bl = split(b)
    return mm(a, bh, dims) + mm(a, bl, dims)


def greet(peers):
    barrier = pltpu.get_barrier_semaphore()
    for axis, peer in peers:
        pl.semaphore_signal(barrier, inc=1, device_id={axis: peer}, device_id_type=MESH)
    return lambda: pl.semaphore_wait(barrier, len(peers))


def send_to(src, dst, send_sem, recv_sem, axis, peer):
    return pltpu.make_async_remote_copy(
        src_ref=src,
        dst_ref=dst,
        send_sem=send_sem,
        recv_sem=recv_sem,
        device_id={axis: peer},
        device_id_type=MESH,
    )


class Gather4:
    def __init__(self, slots, me, right, left, ssem, rsem):
        before, after = lax.rem(me + 3, 4), lax.rem(me + 1, 4)
        self.own = [
            send_to(slots.at[me], slots.at[me], ssem.at[0], rsem.at[0], "seq", right),
            send_to(slots.at[me], slots.at[me], ssem.at[1], rsem.at[1], "seq", left),
        ]
        self.arrive = [
            send_to(slots.at[before], slots.at[before], ssem.at[0], rsem.at[0], "seq", right),
            send_to(slots.at[after], slots.at[after], ssem.at[1], rsem.at[1], "seq", left),
        ]
        self.onward = [
            send_to(
                slots.at[before, 0], slots.at[before, 0], ssem.at[2], rsem.at[2], "seq", right
            ),
            send_to(slots.at[after, 1], slots.at[after, 1], ssem.at[3], rsem.at[3], "seq", left),
        ]
        far = lax.rem(me + 2, 4)
        self.far = [
            send_to(slots.at[far, 0], slots.at[far, 0], ssem.at[2], rsem.at[2], "seq", right),
            send_to(slots.at[far, 1], slots.at[far, 1], ssem.at[3], rsem.at[3], "seq", left),
        ]

    def start(self):
        for copy in self.own:
            copy.start()

    def forward(self):
        for came, on in zip(self.arrive, self.onward):
            came.wait_recv()
            on.start()

    def finish(self):
        for copy in self.far:
            copy.wait_recv()

    def drain(self):
        for copy in self.own + self.onward:
            copy.wait_send()


def compose(later, earlier):
    later = later.astype(F32)
    earlier = earlier.astype(F32)
    joined = mm3(later[:, :DK], earlier)
    return joined + jnp.concatenate([jnp.zeros((DK, DK), F32), later[:, DK:]], axis=1)


def seq_part(q_ref, k_ref, v_ref, g_ref, ld_ref, wr_ref, gain_ref, o_ref, xs, ys, sems, at, meet, late):
    xsend, xrecv, ysend, yrecv = sems
    x, y, x_right, x_left, y_right, y_left = at
    chunks = q_ref.shape[0] // CH
    row = lax.broadcasted_iota(jnp.int32, (CH, CH), 0)
    col = lax.broadcasted_iota(jnp.int32, (CH, CH), 1)
    eye = row == col
    causal = row >= col
    strict = row > col
    pairs = [(n, h) for n in range(chunks) for h in range(2)]

    keys, kk, qk, queries = [], [], [], []
    for n in range(chunks):
        rows = slice(n * CH, (n + 1) * CH)
        k = k_ref[rows, :].astype(F32)
        k = k * lax.rsqrt(jnp.sum(k * k, axis=-1, keepdims=True) + EPS)
        q = q_ref[rows, :].astype(F32)
        q = q * lax.rsqrt(jnp.sum(q * q, axis=-1, keepdims=True) + EPS) * DK ** (-0.5)
        ks = split(k)
        keys.append(k)
        queries.append(q)
        kk.append(mm3(ks, ks, NT))
        qk.append(mm3(split(q), ks, NT))

    decay, grow, tail, end, strict_part, rate = {}, {}, {}, {}, {}, {}
    for n, h in pairs:
        ld_row = ld_ref[h : h + 1, n * CH : (n + 1) * CH]
        ld_all = jnp.broadcast_to(ld_row, (CH, CH))
        wr_all = jnp.broadcast_to(wr_ref[h : h + 1, n * CH : (n + 1) * CH], (CH, CH))
        ld_col = jnp.sum(jnp.where(eye, ld_all, 0.0), axis=1, keepdims=True)
        cum_col = jnp.sum(jnp.where(causal, ld_all, 0.0), axis=1, keepdims=True)
        cum_row = jnp.sum(jnp.where(row <= col, ld_col, 0.0), axis=0, keepdims=True)
        rate[n, h] = jnp.sum(jnp.where(eye, wr_all, 0.0), axis=1, keepdims=True)
        total = jnp.sum(ld_row, axis=1, keepdims=True)
        decay[n, h] = jnp.where(causal, jnp.exp(jnp.where(causal, cum_col - cum_row, 0.0)), 0.0)
        grow[n, h] = jnp.exp(cum_col)
        tail[n, h] = jnp.exp(total - cum_col)
        end[n, h] = jnp.exp(total)
        strict_part[n, h] = jnp.where(strict, kk[n] * decay[n, h] * rate[n, h], 0.0)

    inverse = {}
    for p in pairs:
        low = jnp.where((row // 2 == col // 2) & strict, strict_part[p], 0.0)
        inverse[p] = jnp.where(eye, 1.0, -low)
    width = 2
    while width < CH:
        mask = (row // (2 * width) == col // (2 * width)) & (row // width > col // width)
        inner = {}
        held = {}
        for p in pairs:
            held[p] = split(inverse[p])
            inner[p] = mm3(split(jnp.where(mask, strict_part[p], 0.0)), held[p])
        for p in pairs:
            inverse[p] = inverse[p] - mm3(held[p], split(inner[p]))
        width *= 2

    step, solved = {}, {}
    for n, h in pairs:
        value = v_ref[n * CH : (n + 1) * CH, h * DV : (h + 1) * DV].astype(F32)
        sides = jnp.concatenate([keys[n] * (rate[n, h] * grow[n, h]), value * rate[n, h]], axis=1)
        solved[n, h] = split(mm3(inverse[n, h], sides))
    for n, h in pairs:
        fed = mm3(split(keys[n] * tail[n, h]), solved[n, h], TN)
        step[n, h] = jnp.concatenate(
            [jnp.where(eye, end[n, h], 0.0) - fed[:, :DK], fed[:, DK:]], axis=1
        )

    prefixes = {}
    for h in range(2):
        first = compose(step[1, h], step[0, h])
        second = compose(step[3, h], step[2, h])
        whole = compose(second, first)
        xs[x, h] = whole.astype(BF16)
        prefixes[1, h] = step[0, h]
        prefixes[2, h] = first
        prefixes[3, h] = (step[2, h], first)

    meet()
    along_x = Gather4(xs, x, x_right, x_left, xsend, xrecv)
    along_x.start()

    base, mapped = {}, {}
    for n, h in pairs:
        scores = qk[n] * decay[n, h]
        seen = mm3(split(scores), solved[n, h])
        effective = queries[n] * grow[n, h] - seen[:, :DK]
        if n == 0:
            base[n, h], mapped[n, h] = seen[:, DK:], effective
        else:
            ahead = prefixes[n, h]
            if n == 3:
                ahead = compose(ahead[0], ahead[1])
            through = mm3(effective, ahead)
            base[n, h], mapped[n, h] = seen[:, DK:] + through[:, DK:], through[:, :DK]

    along_x.forward()
    along_x.finish()
    along_y = Gather4(ys, y, y_right, y_left, ysend, yrecv)
    for h in range(2):
        lower = compose(xs[1, h], xs[0, h])
        upper = compose(xs[3, h], xs[2, h])
        ys[y, h] = compose(upper, lower).astype(BF16)
    along_y.start()

    state = {}
    inside = {}
    start = jnp.where(
        lax.broadcasted_iota(jnp.int32, (DK, 2 * DK), 0)
        == lax.broadcasted_iota(jnp.int32, (DK, 2 * DK), 1),
        1.0,
        0.0,
    )
    for h in range(2):
        running = jnp.where(x > 0, xs[0, h].astype(F32), start)
        for other in range(1, 3):
            running = jnp.where(x > other, compose(xs[other, h], running), running)
        inside[h] = running
    along_y.forward()
    along_y.finish()
    for h in range(2):
        running = jnp.where(y > 0, ys[0, h, :, DK:].astype(F32), 0.0)
        for other in range(1, 3):
            after = mm2(ys[other, h, :, :DK], running) + ys[other, h, :, DK:].astype(F32)
            running = jnp.where(y > other, after, running)
        state[h] = split(mm3(inside[h][:, :DK], running) + inside[h][:, DK:])

    late()
    gain = gain_ref[...]
    for n, h in pairs:
        rows, cols = slice(n * CH, (n + 1) * CH), slice(h * DV, (h + 1) * DV)
        readout = base[n, h] + mm3(mapped[n, h], state[h])
        scaled = readout * lax.rsqrt(jnp.mean(readout * readout, axis=-1, keepdims=True) + EPS)
        gate = g_ref[rows, cols].astype(F32)
        o_ref[rows, cols] = (scaled * gain * (gate / (1.0 + jnp.exp(-gate)))).astype(BF16)


    def drain():
        along_x.drain()
        along_y.drain()

    return drain


class RingSum:
    def __init__(self, own, pair_out, pair_in, out, came, psem, rsem, ring):
        self.own, self.pair_out, self.pair_in, self.out, self.came = own, pair_out, pair_in, out, came
        self.psem, self.rsem, self.ring = psem, rsem, ring
        self.sent, self.paired = [], set()

    def pair(self, d):
        return send_to(
            self.pair_out.at[d],
            self.pair_in.at[d],
            self.psem.at[0, d],
            self.psem.at[1, d],
            "exp",
            self.ring[2],
        )

    def offer(self, d):
        copy = self.pair(d)
        copy.start()
        self.sent.append(copy)

    def chip_sum(self, d, half):
        if d not in self.paired:
            self.pair(d).wait_recv()
            self.paired.add(d)
        cols = slice(half * HALF, (half + 1) * HALF)
        return self.own[d, :, cols] + self.pair_in[d, :, cols].astype(F32)

    def hop(self, way, step, half):
        return send_to(
            self.out.at[way, step, half],
            self.came.at[way, step, half],
            self.rsem.at[0, way, step, half],
            self.rsem.at[1, way, step, half],
            "exp",
            self.ring[way],
        )

    def run(self):
        for step in range(4):
            for turn in range(2):
                for way in range(2):
                    half = way if turn == 0 else 1 - way
                    if step == 0 and turn == 1:
                        continue
                    d = 4 - step if way == 0 else 4 + step
                    total = self.chip_sum(d, half)
                    if step >= 2 or (step == 1 and turn == 0):
                        self.hop(way, step - 1, half).wait_recv()
                        total = total + self.came[way, step - 1, half].astype(F32)
                    self.out[way, step, half] = total.astype(BF16)
                    copy = self.hop(way, step, half)
                    copy.start()
                    self.sent.append(copy)

    def result(self, half):
        total = self.chip_sum(0, half)
        for way in range(2):
            self.hop(way, 3, half).wait_recv()
            total = total + self.came[way, 3, half].astype(F32)
        return total

    def drain(self):
        for copy in self.sent:
            copy.wait_send()


def kernel(*refs):
    inputs, o_ref, scratch = refs[:15], refs[15], refs[16:]
    held, scratch = scratch[:15], scratch[15:]
    (own, pair_out, pair_in, out, came, res, low, high, mix_ref, xs, ys) = scratch[:11]
    (wsem, psem, rsem, gsem, bsem, *seq_sems) = scratch[11:]
    (hid_ref, q, k, v, g, ld, wr, gain, ow, post_ref, ids_ref, route_ref, gw, uw, dw) = held
    loads = [
        pltpu.make_async_copy(src, dst, wsem.at[i])
        for i, (src, dst) in enumerate(zip(inputs, held))
    ]
    early, middle = (2, 1, 5, 6, 3), (4, 7, 8, 0, 9, 10, 11)
    for i in early:
        loads[i].start()

    place = lax.axis_index("exp")
    z, core = lax.div(place, 2), lax.rem(place, 2)
    right = lax.rem(z + 1, 8) * 2 + core
    left = lax.rem(z + 7, 8) * 2 + core
    sibling = z * 2 + (1 - core)
    ring = (right, left, sibling)
    turn_at = lax.axis_index("seq")
    x, y = lax.rem(turn_at, 4), lax.div(turn_at, 4)
    at = (
        x,
        y,
        y * 4 + lax.rem(x + 1, 4),
        y * 4 + lax.rem(x + 3, 4),
        lax.rem(y + 1, 4) * 4 + x,
        lax.rem(y + 3, 4) * 4 + x,
    )
    meet = greet([("seq", peer) for peer in at[2:]] + [("exp", peer) for peer in ring])
    for i in early:
        loads[i].wait()
    for i in middle + (12, 13, 14):
        loads[i].start()

    def late():
        for i in middle:
            loads[i].wait()

    drain_seq = seq_part(q, k, v, g, ld, wr, gain, mix_ref, xs, ys, seq_sems, at, meet, late)

    first = RingSum(
        own.at[0],
        pair_out.at[0],
        pair_in.at[0],
        out.at[0],
        came.at[0],
        psem.at[0],
        rsem.at[0],
        ring,
    )
    weight = ow[...]
    for d in (4, 3, 5, 2, 6, 1, 7, 0):
        chip = lax.rem(z + d, 8)
        for mine in (False, True):
            part = core if mine else 1 - core
            rows = pl.ds(pl.multiple_of(chip * 64 + part * 32, 32), 32)
            block = mm(mix_ref[rows, :], weight)
            if mine:
                own[0, d] = block
            else:
                pair_out[0, d] = block.astype(BF16)
                first.offer(d)
    first.run()
    for half in range(2):
        cols = slice(half * HALF, (half + 1) * HALF)
        res[:, cols] = hid_ref[:, cols].astype(F32) + first.result(half)

    residual = res[...]
    normed = (
        residual
        * lax.rsqrt(jnp.mean(residual * residual, axis=-1, keepdims=True) + EPS)
        * post_ref[...]
    ).astype(BF16)
    low[0, 0, :, :HALF] = normed[:, :HALF]
    high[0, 0] = normed[:, HALF:]
    lane = lax.broadcasted_iota(jnp.int32, (32, 128), 1)
    table = jnp.zeros((32, 128), F32)
    ids = ids_ref[...].astype(F32)
    routes = route_ref[...].astype(F32)
    same = lax.broadcasted_iota(jnp.int32, (32, 32), 0) == lax.broadcasted_iota(
        jnp.int32, (32, 32), 1
    )
    for j in range(4):
        named, share = (
            jnp.sum(jnp.where(same, a[j : j + 1, :], 0.0), axis=1, keepdims=True)
            for a in (ids, routes)
        )
        table = table + jnp.where(lane.astype(F32) == named, share, 0.0)
    low[0, 0, :, HALF:] = table.astype(BF16)

    halves = (low, high)
    sent = []

    def onward(way, step, half):
        src = (8 - step) % 8 if way == 0 else step
        dst = 7 - step if way == 0 else step + 1
        return send_to(
            halves[half].at[src, 0],
            halves[half].at[dst, 0],
            gsem.at[0, way, step, half],
            gsem.at[1, way, step, half],
            "exp",
            ring[way],
        )

    def across(d, half):
        return send_to(
            halves[half].at[d, 0],
            halves[half].at[d, 1],
            bsem.at[0, d, half],
            bsem.at[1, d, half],
            "exp",
            sibling,
        )

    def begin(copy):
        copy.start()
        sent.append(copy)

    second = RingSum(
        own.at[1],
        pair_out.at[1],
        pair_in.at[1],
        out.at[1],
        came.at[1],
        psem.at[1],
        rsem.at[1],
        ring,
    )

    def expert(offsets):
        for d in offsets:
            for half in range(2):
                across(d, half).wait_recv()
        cells = [(d, side) for d in offsets for side in range(2)]
        left_part = jnp.concatenate([low[d, side, :, :HALF] for d, side in cells], axis=0)
        right_part = jnp.concatenate([high[d, side] for d, side in cells], axis=0)
        gate = mm(left_part, gw[0, :HALF, :]) + mm(right_part, gw[0, HALF:, :])
        up = mm(left_part, uw[0, :HALF, :]) + mm(right_part, uw[0, HALF:, :])
        hidden = (gate / (1.0 + jnp.exp(-gate)) * up).astype(BF16)
        produced = mm(hidden, dw[0]).astype(BF16).astype(F32)
        for i, (d, side) in enumerate(cells):
            share = jnp.sum(
                jnp.where(lane == place, low[d, side, :, HALF:].astype(F32), 0.0),
                axis=1,
                keepdims=True,
            )
            block = produced[32 * i : 32 * i + 32] * share
            if side == 0:
                own[1, d] = block
            else:
                pair_out[1, d] = block.astype(BF16)
                second.offer(d)

    for way in range(2):
        for half in (way, 1 - way):
            begin(onward(way, 0, half))
    for half in range(2):
        begin(across(0, half))
    for load in loads[12:]:
        load.wait()
    expert((0,))
    for step in range(1, 4):
        for turn in range(2):
            for way in range(2):
                half = way if turn == 0 else 1 - way
                onward(way, step - 1, half).wait_recv()
                if step < 3 or turn == 0:
                    begin(onward(way, step, half))
                begin(across(8 - step if way == 0 else step, half))
        expert((8 - step, step))
    for way in range(2):
        onward(way, 3, way).wait_recv()
        begin(across(4, way))
    expert((4,))
    second.run()
    for half in range(2):
        cols = slice(half * HALF, (half + 1) * HALF)
        o_ref[:, cols] = (res[:, cols] + second.result(half)).astype(BF16)
    for copy in sent:
        copy.wait_send()
    first.drain()
    second.drain()
    drain_seq()


def per_device(*args):
    args = list(args)
    args[7] = args[7].reshape(1, DV)
    args[9] = args[9].reshape(1, D)
    args[10] = args[10].T
    args[11] = args[11].T
    slots = pltpu.VMEM((4, 2, DK, 2 * DK), BF16)
    scratch = [pltpu.VMEM(a.shape, a.dtype) for a in args] + [
        pltpu.VMEM((2, 8, 32, D), F32),
        pltpu.VMEM((2, 8, 32, D), BF16),
        pltpu.VMEM((2, 8, 32, D), BF16),
        pltpu.VMEM((2, 2, 4, 2, 32, HALF), BF16),
        pltpu.VMEM((2, 2, 4, 2, 32, HALF), BF16),
        pltpu.VMEM((32, D), F32),
        pltpu.VMEM((8, 2, 32, HALF + 128), BF16),
        pltpu.VMEM((8, 2, 32, HALF), BF16),
        pltpu.VMEM(args[3].shape, BF16),
        slots,
        slots,
        pltpu.SemaphoreType.DMA((15,)),
        pltpu.SemaphoreType.DMA((2, 2, 8)),
        pltpu.SemaphoreType.DMA((2, 2, 2, 4, 2)),
        pltpu.SemaphoreType.DMA((2, 2, 4, 2)),
        pltpu.SemaphoreType.DMA((2, 8, 2)),
    ]
    return pl.pallas_call(
        kernel,
        out_shape=jax.ShapeDtypeStruct(args[0].shape, BF16),
        in_specs=[pl.BlockSpec(memory_space=pl.ANY)] * 15,
        out_specs=pl.BlockSpec(memory_space=pltpu.VMEM),
        scratch_shapes=scratch + [pltpu.SemaphoreType.DMA((4,))] * 4,
        compiler_params=pltpu.CompilerParams(
            collective_id=0, has_side_effects=True, vmem_limit_bytes=62 * 1024 * 1024
        ),
        name="layer",
    )(*args)


def solution(mesh):
    in_specs = (
        P(("seq", "exp"), None),
        P("seq", "exp"),
        P("seq", "exp"),
        P("seq", "exp"),
        P("seq", "exp"),
        P("exp", "seq"),
        P("exp", "seq"),
        P(),
        P("exp", None),
        P(),
        P(("seq", "exp"), None),
        P(("seq", "exp"), None),
        P("exp", None, None),
        P("exp", None, None),
        P("exp", None, None),
    )
    out_specs = P(("seq", "exp"), None)
    return jax.shard_map(
        per_device, mesh=mesh, in_specs=in_specs, out_specs=out_specs, check_vma=False
    )
```

```python
import functools

import jax
import jax.numpy as jnp
from jax import lax
from jax.experimental import pallas as pl
from jax.experimental.pallas import tpu as pltpu
from jax.sharding import PartitionSpec as P

D = 2048
FF = 512
DK = 128
DV = 128
EPS = 1e-06
CH = 128
PARTS = 4
WIDE = D // PARTS
F32 = jnp.float32
BF16 = jnp.bfloat16
MESH = pl.DeviceIdType.MESH
NN = (((1,), (0,)), ((), ()))
NT = (((1,), (1,)), ((), ()))
TN = (((0,), (0,)), ((), ()))


def mm(a, b, dims=NN):
    return lax.dot_general(a, b, dims, preferred_element_type=F32)


def split(a):
    hi = a.astype(BF16)
    return hi, (a - hi.astype(F32)).astype(BF16)


def mm3(a, b, dims=NN):
    ah, al = a if isinstance(a, tuple) else split(a)
    bh, bl = b if isinstance(b, tuple) else split(b)
    return mm(ah, bh, dims) + (mm(ah, bl, dims) + mm(al, bh, dims))


def mm2(a, b, dims=NN):
    bh, bl = split(b)
    return mm(a, bh, dims) + mm(a, bl, dims)


def greet(peers):
    barrier = pltpu.get_barrier_semaphore()
    for axis, peer in peers:
        pl.semaphore_signal(barrier, inc=1, device_id={axis: peer}, device_id_type=MESH)
    return lambda: pl.semaphore_wait(barrier, len(peers))


def send_to(src, dst, send_sem, recv_sem, axis, peer):
    return pltpu.make_async_remote_copy(
        src_ref=src,
        dst_ref=dst,
        send_sem=send_sem,
        recv_sem=recv_sem,
        device_id={axis: peer},
        device_id_type=MESH,
    )


class Gather4:
    def __init__(self, slots, me, right, left, ssem, rsem):
        before, after = lax.rem(me + 3, 4), lax.rem(me + 1, 4)
        self.own = [
            send_to(slots.at[me], slots.at[me], ssem.at[0], rsem.at[0], "seq", right),
            send_to(slots.at[me], slots.at[me], ssem.at[1], rsem.at[1], "seq", left),
        ]
        self.arrive = [
            send_to(slots.at[before], slots.at[before], ssem.at[0], rsem.at[0], "seq", right),
            send_to(slots.at[after], slots.at[after], ssem.at[1], rsem.at[1], "seq", left),
        ]
        self.onward = [
            send_to(
                slots.at[before, 0], slots.at[before, 0], ssem.at[2], rsem.at[2], "seq", right
            ),
            send_to(slots.at[after, 1], slots.at[after, 1], ssem.at[3], rsem.at[3], "seq", left),
        ]
        far = lax.rem(me + 2, 4)
        self.far = [
            send_to(slots.at[far, 0], slots.at[far, 0], ssem.at[2], rsem.at[2], "seq", right),
            send_to(slots.at[far, 1], slots.at[far, 1], ssem.at[3], rsem.at[3], "seq", left),
        ]

    def start(self):
        for copy in self.own:
            copy.start()

    def forward(self):
        for came, on in zip(self.arrive, self.onward):
            came.wait_recv()
            on.start()

    def finish(self):
        for copy in self.far:
            copy.wait_recv()

    def drain(self):
        for copy in self.own + self.onward:
            copy.wait_send()


def compose(later, earlier):
    later = later.astype(F32)
    earlier = earlier.astype(F32)
    joined = mm3(later[:, :DK], earlier)
    return joined + jnp.concatenate([jnp.zeros((DK, DK), F32), later[:, DK:]], axis=1)


def seq_part(q_ref, k_ref, v_ref, g_ref, ld_ref, wr_ref, gain_ref, mix, xs, ys, sems, at, late, ready):
    xsend, xrecv, ysend, yrecv = sems
    x, y, x_right, x_left, y_right, y_left = at
    chunks = q_ref.shape[0] // CH
    row = lax.broadcasted_iota(jnp.int32, (CH, CH), 0)
    col = lax.broadcasted_iota(jnp.int32, (CH, CH), 1)
    eye = row == col
    causal = row >= col
    strict = row > col
    pairs = [(n, h) for n in range(chunks) for h in range(2)]

    keys, kk, qk, queries = [], [], [], []
    for n in range(chunks):
        rows = slice(n * CH, (n + 1) * CH)
        k = k_ref[rows, :].astype(F32)
        k = k * lax.rsqrt(jnp.sum(k * k, axis=-1, keepdims=True) + EPS)
        q = q_ref[rows, :].astype(F32)
        q = q * lax.rsqrt(jnp.sum(q * q, axis=-1, keepdims=True) + EPS) * DK ** (-0.5)
        ks = split(k)
        keys.append(k)
        queries.append(q)
        kk.append(mm3(ks, ks, NT))
        qk.append(mm3(split(q), ks, NT))

    decay, grow, tail, end, strict_part, rate = {}, {}, {}, {}, {}, {}
    for n, h in pairs:
        ld_row = ld_ref[h : h + 1, n * CH : (n + 1) * CH]
        ld_all = jnp.broadcast_to(ld_row, (CH, CH))
        wr_all = jnp.broadcast_to(wr_ref[h : h + 1, n * CH : (n + 1) * CH], (CH, CH))
        ld_col = jnp.sum(jnp.where(eye, ld_all, 0.0), axis=1, keepdims=True)
        cum_col = jnp.sum(jnp.where(causal, ld_all, 0.0), axis=1, keepdims=True)
        cum_row = jnp.sum(jnp.where(row <= col, ld_col, 0.0), axis=0, keepdims=True)
        rate[n, h] = jnp.sum(jnp.where(eye, wr_all, 0.0), axis=1, keepdims=True)
        total = jnp.sum(ld_row, axis=1, keepdims=True)
        decay[n, h] = jnp.where(causal, jnp.exp(jnp.where(causal, cum_col - cum_row, 0.0)), 0.0)
        grow[n, h] = jnp.exp(cum_col)
        tail[n, h] = jnp.exp(total - cum_col)
        end[n, h] = jnp.exp(total)
        strict_part[n, h] = jnp.where(strict, kk[n] * decay[n, h] * rate[n, h], 0.0)

    inverse = {}
    for p in pairs:
        low = jnp.where((row // 2 == col // 2) & strict, strict_part[p], 0.0)
        inverse[p] = jnp.where(eye, 1.0, -low)
    width = 2
    while width < CH:
        mask = (row // (2 * width) == col // (2 * width)) & (row // width > col // width)
        inner = {}
        held = {}
        for p in pairs:
            held[p] = split(inverse[p])
            inner[p] = mm3(split(jnp.where(mask, strict_part[p], 0.0)), held[p])
        for p in pairs:
            inverse[p] = inverse[p] - mm3(held[p], split(inner[p]))
        width *= 2

    step, solved = {}, {}
    for n, h in pairs:
        value = v_ref[n * CH : (n + 1) * CH, h * DV : (h + 1) * DV].astype(F32)
        sides = jnp.concatenate([keys[n] * (rate[n, h] * grow[n, h]), value * rate[n, h]], axis=1)
        solved[n, h] = split(mm3(inverse[n, h], sides))
    for n, h in pairs:
        fed = mm3(split(keys[n] * tail[n, h]), solved[n, h], TN)
        step[n, h] = jnp.concatenate(
            [jnp.where(eye, end[n, h], 0.0) - fed[:, :DK], fed[:, DK:]], axis=1
        )

    prefixes = {}
    for h in range(2):
        first = compose(step[1, h], step[0, h])
        second = compose(step[3, h], step[2, h])
        whole = compose(second, first)
        xs[x, h] = whole.astype(BF16)
        prefixes[1, h] = step[0, h]
        prefixes[2, h] = first
        prefixes[3, h] = (step[2, h], first)

    along_x = Gather4(xs, x, x_right, x_left, xsend, xrecv)
    along_x.start()

    base, mapped = {}, {}
    for n, h in pairs:
        scores = qk[n] * decay[n, h]
        seen = mm3(split(scores), solved[n, h])
        effective = queries[n] * grow[n, h] - seen[:, :DK]
        if n == 0:
            base[n, h], mapped[n, h] = seen[:, DK:], effective
        else:
            ahead = prefixes[n, h]
            if n == 3:
                ahead = compose(ahead[0], ahead[1])
            through = mm3(effective, ahead)
            base[n, h], mapped[n, h] = seen[:, DK:] + through[:, DK:], through[:, :DK]

    along_x.forward()
    along_x.finish()
    along_y = Gather4(ys, y, y_right, y_left, ysend, yrecv)
    for h in range(2):
        lower = compose(xs[1, h], xs[0, h])
        upper = compose(xs[3, h], xs[2, h])
        ys[y, h] = compose(upper, lower).astype(BF16)
    along_y.start()

    state = {}
    inside = {}
    start = jnp.where(
        lax.broadcasted_iota(jnp.int32, (DK, 2 * DK), 0)
        == lax.broadcasted_iota(jnp.int32, (DK, 2 * DK), 1),
        1.0,
        0.0,
    )
    for h in range(2):
        running = jnp.where(x > 0, xs[0, h].astype(F32), start)
        for other in range(1, 3):
            running = jnp.where(x > other, compose(xs[other, h], running), running)
        inside[h] = running
    along_y.forward()
    along_y.finish()
    for h in range(2):
        running = jnp.where(y > 0, ys[0, h, :, DK:].astype(F32), 0.0)
        for other in range(1, 3):
            after = mm2(ys[other, h, :, :DK], running) + ys[other, h, :, DK:].astype(F32)
            running = jnp.where(y > other, after, running)
        state[h] = split(mm3(inside[h][:, :DK], running) + inside[h][:, DK:])

    late()
    gain = gain_ref[...]
    for h in range(2):
        cols = slice(h * DV, (h + 1) * DV)
        for n in range(chunks):
            rows = slice(n * CH, (n + 1) * CH)
            readout = base[n, h] + mm3(mapped[n, h], state[h])
            scaled = readout * lax.rsqrt(jnp.mean(readout * readout, axis=-1, keepdims=True) + EPS)
            gate = g_ref[rows, cols].astype(F32)
            mixed = (scaled * gain * (gate / (1.0 + jnp.exp(-gate)))).astype(BF16)
            for i in range(4):
                at_chip = (2 * n + i // 2) * 32
                mix[i % 2, h, at_chip : at_chip + 32] = mixed[32 * i : 32 * i + 32]
        ready(h)

    def drain():
        along_x.drain()
        along_y.drain()

    return drain


class RingSum:
    def __init__(self, own, out, came, sem, ring):
        self.own, self.out, self.came, self.sem, self.ring = own, out, came, sem, ring
        self.sent = []

    def hop(self, way, step, part):
        return send_to(
            self.out.at[way, step, part],
            self.came.at[way, step, part],
            self.sem.at[0, way, step, part],
            self.sem.at[1, way, step, part],
            "exp",
            self.ring[way],
        )

    def run(self, prepare):
        for step in range(4):
            prepare(step)
            for turn, way, part in turns():
                if step == 0 and turn == 1:
                    continue
                d = 4 - step if way == 0 else 4 + step
                total = self.own[d, :, part * WIDE : (part + 1) * WIDE]
                if step >= 2 or (step == 1 and turn == 0):
                    self.hop(way, step - 1, part).wait_recv()
                    total = total + self.came[way, step - 1, part].astype(F32)
                self.out[way, step, part] = total.astype(BF16)
                copy = self.hop(way, step, part)
                copy.start()
                self.sent.append(copy)
        prepare(4)

    def result(self, part):
        total = self.own[0, :, part * WIDE : (part + 1) * WIDE]
        for way in range(2):
            self.hop(way, 3, part).wait_recv()
            total = total + self.came[way, 3, part].astype(F32)
        return total

    def drain(self):
        for copy in self.sent:
            copy.wait_send()


def turns():
    some = PARTS // 2
    return [
        (turn, way, (way if turn == 0 else 1 - way) * some + i)
        for turn in range(2)
        for i in range(some)
        for way in range(2)
    ]


def kernel(*refs):
    inputs, o_ref, scratch = refs[:15], refs[15], refs[16:]
    held, scratch = scratch[:15], scratch[15:]
    (own, out, came, res, tokens, table, mix, mix_in, xs, ys) = scratch[:10]
    (wsem, csem, msem, tsem, rsem, gsem, *seq_sems) = scratch[10:]
    (hid_ref, q, k, v, g, ld, wr, gain, ow, post_ref, ids_ref, route_ref, gw, uw, dw) = held
    weights = (8, 12, 13, 14)

    place = lax.axis_index("exp")
    z, core = lax.div(place, 2), lax.rem(place, 2)
    chips = [lax.rem(z + d, 8) * 2 + core for d in range(8)]
    sibling = z * 2 + (1 - core)
    ring = (chips[1], chips[7])
    turn_at = lax.axis_index("seq")
    x, y = lax.rem(turn_at, 4), lax.div(turn_at, 4)
    at = (
        x,
        y,
        y * 4 + lax.rem(x + 1, 4),
        y * 4 + lax.rem(x + 3, 4),
        lax.rem(y + 1, 4) * 4 + x,
        lax.rem(y + 3, 4) * 4 + x,
    )
    meet = greet(
        [("seq", peer) for peer in at[2:]] + [("exp", peer) for peer in chips[1:] + [sibling]]
    )

    loads, shared = [], []
    for i, (src, dst) in enumerate(zip(inputs, held)):
        if i in weights:
            flat = src if i == 8 else src.at[0]
            n = weights.index(i)
            shared.append(
                send_to(flat, dst.at[core], csem.at[0, n], csem.at[1, n], "exp", sibling)
            )
            dst, src = dst.at[core], flat
        loads.append(pltpu.make_async_copy(src, dst, wsem.at[i]))
    arriving = [
        send_to(
            held[i].at[1 - core], held[i].at[1 - core], csem.at[0, n], csem.at[1, n], "exp", sibling
        )
        for n, i in enumerate(weights)
    ]
    early, middle = (2, 1, 5, 6, 3), (10, 11, 4, 7, 0, 9)
    for i in early + middle:
        loads[i].start()
    meet()
    for i in early:
        loads[i].wait()
    for i in weights:
        loads[i].start()
    for copy in shared:
        copy.start()

    lane = lax.broadcasted_iota(jnp.int32, (32, 128), 1).astype(F32)
    sent = []

    def begin(copy):
        copy.start()
        sent.append(copy)

    def late():
        for i in middle:
            loads[i].wait()
        ids = ids_ref[...].astype(F32)
        routes = route_ref[...].astype(F32)
        same = lax.broadcasted_iota(jnp.int32, (32, 32), 0) == lax.broadcasted_iota(
            jnp.int32, (32, 32), 1
        )
        shares = jnp.zeros((32, 128), F32)
        for j in range(4):
            named, share = (
                jnp.sum(jnp.where(same, a[j : j + 1, :], 0.0), axis=1, keepdims=True)
                for a in (ids, routes)
            )
            shares = shares + jnp.where(lane == named, share, 0.0)
        table[0] = shares.astype(BF16)
        for d in range(1, 8):
            begin(share_table(d))

    def share_table(d):
        return send_to(
            table.at[0], table.at[8 - d], tsem.at[0, 8 - d], tsem.at[1, 8 - d], "exp", chips[d]
        )

    def mix_copy(h):
        return send_to(
            mix.at[1 - core, h], mix_in.at[h], msem.at[0, h], msem.at[1, h], "exp", sibling
        )

    drain_seq = seq_part(
        q,
        k,
        v,
        g,
        ld,
        wr,
        gain,
        mix,
        xs,
        ys,
        seq_sems,
        at,
        late,
        lambda h: begin(mix_copy(h)),
    )

    loads[8].wait()
    arriving[0].wait_recv()
    for h in range(2):
        mix_copy(h).wait_recv()

    def project(offsets):
        rows = [pl.ds(pl.multiple_of(lax.rem(z + d, 8) * 32, 32), 32) for d in offsets]
        mine, other = (
            jnp.concatenate(
                [jnp.concatenate([ref[h, r] for h in range(2)], axis=1) for r in rows], axis=0
            )
            for ref in (mix.at[core], mix_in)
        )
        block = mm(mine, ow[core]) + mm(other, ow[1 - core])
        for i, d in enumerate(offsets):
            own[0, d] = block[32 * i : 32 * i + 32]

    first = RingSum(own.at[0], out.at[0], came.at[0], rsem.at[0], ring)
    first.run(lambda step: project(((4,), (3, 5), (2, 6), (1, 7), (0,))[step]))
    for part in range(PARTS):
        cols = slice(part * WIDE, (part + 1) * WIDE)
        res[:, cols] = hid_ref[:, cols].astype(F32) + first.result(part)

    residual = res[...]
    normed = (
        residual
        * lax.rsqrt(jnp.mean(residual * residual, axis=-1, keepdims=True) + EPS)
        * post_ref[...]
    ).astype(BF16)
    for part in range(PARTS):
        tokens[0, part] = normed[:, part * WIDE : (part + 1) * WIDE]

    def onward(way, step, part):
        src = (8 - step) % 8 if way == 0 else step
        dst = 7 - step if way == 0 else step + 1
        return send_to(
            tokens.at[src, part],
            tokens.at[dst, part],
            gsem.at[0, way, step, part],
            gsem.at[1, way, step, part],
            "exp",
            ring[way],
        )

    def expert(offsets):
        picked = jnp.concatenate(
            [
                jnp.concatenate([tokens[d, part] for part in range(PARTS)], axis=1)
                for d in offsets
            ],
            axis=0,
        )
        for d in offsets:
            if d > 0:
                share_table(8 - d).wait_recv()
        shares = jnp.concatenate([table[d] for d in offsets], axis=0).astype(F32)
        lanes = lax.broadcasted_iota(jnp.int32, shares.shape, 1)
        total = None
        for e in range(2):
            gate = mm(picked, gw[e])
            up = mm(picked, uw[e])
            hidden = (gate / (1.0 + jnp.exp(-gate)) * up).astype(BF16)
            produced = mm(hidden, dw[e]).astype(BF16).astype(F32)
            share = jnp.sum(jnp.where(lanes == z * 2 + e, shares, 0.0), axis=1, keepdims=True)
            total = produced * share if total is None else total + produced * share
        for i, d in enumerate(offsets):
            own[1, d] = total[32 * i : 32 * i + 32]

    for turn, way, part in turns():
        begin(onward(way, 0, part))
    for i in weights[1:]:
        loads[i].wait()
    for copy in arriving[1:]:
        copy.wait_recv()
    for step in range(1, 4):
        for turn, way, part in turns():
            onward(way, step - 1, part).wait_recv()
            if step < 3 or turn == 0:
                begin(onward(way, step, part))
        if step == 1:
            expert((0, 1, 7))
        elif step == 2:
            expert((2, 6))
    for turn, way, part in turns():
        if turn == 0:
            onward(way, 3, part).wait_recv()
    expert((3, 4, 5))
    second = RingSum(own.at[1], out.at[1], came.at[1], rsem.at[1], ring)
    second.run(lambda step: None)
    for part in range(PARTS):
        cols = slice(part * WIDE, (part + 1) * WIDE)
        o_ref[:, cols] = (res[:, cols] + second.result(part)).astype(BF16)
    for copy in sent + shared:
        copy.wait_send()
    first.drain()
    second.drain()
    drain_seq()


def per_device(*args):
    args = list(args)
    args[7] = args[7].reshape(1, DV)
    args[9] = args[9].reshape(1, D)
    args[10] = args[10].T
    args[11] = args[11].T
    slots = pltpu.VMEM((4, 2, DK, 2 * DK), BF16)
    both = {8: (2,) + args[8].shape}
    for i in (12, 13, 14):
        both[i] = (2,) + args[i].shape[1:]
    scratch = [pltpu.VMEM(both.get(i, a.shape), a.dtype) for i, a in enumerate(args)] + [
        pltpu.VMEM((2, 8, 32, D), F32),
        pltpu.VMEM((2, 2, 4, PARTS, 32, WIDE), BF16),
        pltpu.VMEM((2, 2, 4, PARTS, 32, WIDE), BF16),
        pltpu.VMEM((32, D), F32),
        pltpu.VMEM((8, PARTS, 32, WIDE), BF16),
        pltpu.VMEM((8, 32, 128), BF16),
        pltpu.VMEM((2, 2, 256, DV), BF16),
        pltpu.VMEM((2, 256, DV), BF16),
        slots,
        slots,
        pltpu.SemaphoreType.DMA((15,)),
        pltpu.SemaphoreType.DMA((2, 4)),
        pltpu.SemaphoreType.DMA((2, 2)),
        pltpu.SemaphoreType.DMA((2, 8)),
        pltpu.SemaphoreType.DMA((2, 2, 2, 4, PARTS)),
        pltpu.SemaphoreType.DMA((2, 2, 4, PARTS)),
    ]
    return pl.pallas_call(
        kernel,
        out_shape=jax.ShapeDtypeStruct(args[0].shape, BF16),
        in_specs=[pl.BlockSpec(memory_space=pl.ANY)] * 15,
        out_specs=pl.BlockSpec(memory_space=pltpu.VMEM),
        scratch_shapes=scratch + [pltpu.SemaphoreType.DMA((4,))] * 4,
        compiler_params=pltpu.CompilerParams(
            collective_id=0, has_side_effects=True, vmem_limit_bytes=62 * 1024 * 1024
        ),
        name="layer",
    )(*args)


def solution(mesh):
    in_specs = (
        P(("seq", "exp"), None),
        P("seq", "exp"),
        P("seq", "exp"),
        P("seq", "exp"),
        P("seq", "exp"),
        P("exp", "seq"),
        P("exp", "seq"),
        P(),
        P("exp", None),
        P(),
        P(("seq", "exp"), None),
        P(("seq", "exp"), None),
        P("exp", None, None),
        P("exp", None, None),
        P("exp", None, None),
    )
    out_specs = P(("seq", "exp"), None)
    return jax.shard_map(
        per_device, mesh=mesh, in_specs=in_specs, out_specs=out_specs, check_vma=False
    )
```

```python
import functools

import jax
import jax.numpy as jnp
from jax import lax
from jax.experimental import pallas as pl
from jax.experimental.pallas import tpu as pltpu
from jax.sharding import PartitionSpec as P

D = 2048
FF = 512
DK = 128
DV = 128
EPS = 1e-06
CH = 128
PARTS = 4
WIDE = D // PARTS
F32 = jnp.float32
BF16 = jnp.bfloat16
MESH = pl.DeviceIdType.MESH
NN = (((1,), (0,)), ((), ()))
NT = (((1,), (1,)), ((), ()))
TN = (((0,), (0,)), ((), ()))


def mm(a, b, dims=NN):
    return lax.dot_general(a, b, dims, preferred_element_type=F32)


def split(a):
    hi = a.astype(BF16)
    return hi, (a - hi.astype(F32)).astype(BF16)


def mm3(a, b, dims=NN):
    ah, al = a if isinstance(a, tuple) else split(a)
    bh, bl = b if isinstance(b, tuple) else split(b)
    if dims != NN:
        return mm(ah, bh, dims) + (mm(ah, bl, dims) + mm(al, bh, dims))
    n = bh.shape[1]
    left = jnp.concatenate([ah, al], axis=1)
    if n > 128:
        return mm(left, jnp.concatenate([bh, bh], axis=0)) + mm(ah, bl)
    right = jnp.concatenate(
        [
            jnp.concatenate([bh, bl], axis=1),
            jnp.concatenate([bh, jnp.zeros_like(bl)], axis=1),
        ],
        axis=0,
    )
    both = mm(left, right)
    return both[:, :n] + both[:, n:]


def mm2(a, b, dims=NN):
    bh, bl = split(b)
    return mm(a, bh, dims) + mm(a, bl, dims)


def greet(peers):
    barrier = pltpu.get_barrier_semaphore()
    for axis, peer in peers:
        pl.semaphore_signal(barrier, inc=1, device_id={axis: peer}, device_id_type=MESH)
    return lambda: pl.semaphore_wait(barrier, len(peers))


def send_to(src, dst, send_sem, recv_sem, axis, peer):
    return pltpu.make_async_remote_copy(
        src_ref=src,
        dst_ref=dst,
        send_sem=send_sem,
        recv_sem=recv_sem,
        device_id={axis: peer},
        device_id_type=MESH,
    )


class Gather4:
    def __init__(self, slots, me, peers, ssem, rsem):
        self.slots, self.me, self.peers, self.ssem, self.rsem = slots, me, peers, ssem, rsem
        self.sent = []

    def copy(self, d, h, i):
        place = lax.rem(self.me + d, 4)
        piece = self.slots.at[place, h, pl.ds(i * 64, 64)]
        return piece, h * 2 + i

    def start(self, h):
        for i in range(2):
            piece, at = self.copy(0, h, i)
            for d in (2, 1, 3):
                copy = send_to(
                    piece, piece, self.ssem.at[d, at], self.rsem.at[d, at], "seq", self.peers[d]
                )
                copy.start()
                self.sent.append(copy)

    def finish(self, h):
        for d in (1, 3, 2):
            for i in range(2):
                piece, at = self.copy(4 - d, h, i)
                send_to(
                    piece, piece, self.ssem.at[d, at], self.rsem.at[d, at], "seq", self.peers[d]
                ).wait_recv()

    def drain(self):
        for copy in self.sent:
            copy.wait_send()


def compose(later, earlier):
    later = later.astype(F32)
    earlier = earlier.astype(F32)
    joined = mm3(later[:, :DK], earlier)
    return joined + jnp.concatenate([jnp.zeros((DK, DK), F32), later[:, DK:]], axis=1)


def seq_part(q_ref, k_ref, v_ref, g_ref, ld_ref, wr_ref, gain_ref, mix, xs, ys, sems, at, meet, late, ready):
    xsend, xrecv, ysend, yrecv = sems
    x, y, x_peers, y_peers = at
    chunks = q_ref.shape[0] // CH
    row = lax.broadcasted_iota(jnp.int32, (CH, CH), 0)
    col = lax.broadcasted_iota(jnp.int32, (CH, CH), 1)
    eye = row == col
    causal = row >= col
    strict = row > col
    pairs = [(n, h) for n in range(chunks) for h in range(2)]

    keys, kk, qk, queries = [], [], [], []
    for n in range(chunks):
        rows = slice(n * CH, (n + 1) * CH)
        k = k_ref[rows, :].astype(F32)
        k = k * lax.rsqrt(jnp.sum(k * k, axis=-1, keepdims=True) + EPS)
        ks = split(k)
        keys.append(k)
        kk.append(mm3(ks, ks, NT))

    decay, grow, tail, end, strict_part, rate = {}, {}, {}, {}, {}, {}
    for n, h in pairs:
        ld_row = ld_ref[h : h + 1, n * CH : (n + 1) * CH]
        ld_all = jnp.broadcast_to(ld_row, (CH, CH))
        wr_all = jnp.broadcast_to(wr_ref[h : h + 1, n * CH : (n + 1) * CH], (CH, CH))
        ld_col = jnp.sum(jnp.where(eye, ld_all, 0.0), axis=1, keepdims=True)
        cum_col = jnp.sum(jnp.where(causal, ld_all, 0.0), axis=1, keepdims=True)
        cum_row = jnp.sum(jnp.where(row <= col, ld_col, 0.0), axis=0, keepdims=True)
        rate[n, h] = jnp.sum(jnp.where(eye, wr_all, 0.0), axis=1, keepdims=True)
        total = jnp.sum(ld_row, axis=1, keepdims=True)
        decay[n, h] = jnp.where(causal, jnp.exp(jnp.where(causal, cum_col - cum_row, 0.0)), 0.0)
        grow[n, h] = jnp.exp(cum_col)
        tail[n, h] = jnp.exp(total - cum_col)
        end[n, h] = jnp.exp(total)
        strict_part[n, h] = jnp.where(strict, kk[n] * decay[n, h] * rate[n, h], 0.0)

    inverse = {}
    for p in pairs:
        low = jnp.where((row // 2 == col // 2) & strict, strict_part[p], 0.0)
        inverse[p] = jnp.where(eye, 1.0, -low)
    width = 2
    while width < CH:
        mask = (row // (2 * width) == col // (2 * width)) & (row // width > col // width)
        inner = {}
        held = {}
        for p in pairs:
            held[p] = split(inverse[p])
            inner[p] = mm3(split(jnp.where(mask, strict_part[p], 0.0)), held[p])
        for p in pairs:
            inverse[p] = inverse[p] - mm3(held[p], split(inner[p]))
        width *= 2

    step, solved = {}, {}
    for n, h in pairs:
        value = v_ref[n * CH : (n + 1) * CH, h * DV : (h + 1) * DV].astype(F32)
        sides = jnp.concatenate([keys[n] * (rate[n, h] * grow[n, h]), value * rate[n, h]], axis=1)
        solved[n, h] = split(mm3(inverse[n, h], sides))
    for n, h in pairs:
        fed = mm3(split(keys[n] * tail[n, h]), solved[n, h], TN)
        step[n, h] = jnp.concatenate(
            [jnp.where(eye, end[n, h], 0.0) - fed[:, :DK], fed[:, DK:]], axis=1
        )

    along_x = Gather4(xs, x, x_peers, xsend, xrecv)
    along_y = Gather4(ys, y, y_peers, ysend, yrecv)
    prefixes = {}
    for h in range(2):
        first = compose(step[1, h], step[0, h])
        second = compose(step[3, h], step[2, h])
        whole = compose(second, first)
        xs[x, h] = whole.astype(BF16)
        if h == 0:
            meet()
        along_x.start(h)
        prefixes[1, h] = step[0, h]
        prefixes[2, h] = first
        prefixes[3, h] = (step[2, h], first)
    late()

    base, mapped = {}, {}
    for n in range(chunks):
        q = q_ref[n * CH : (n + 1) * CH, :].astype(F32)
        q = q * lax.rsqrt(jnp.sum(q * q, axis=-1, keepdims=True) + EPS) * DK ** (-0.5)
        queries.append(q)
        qk.append(mm3(split(q), split(keys[n]), NT))
    for n, h in pairs:
        scores = qk[n] * decay[n, h]
        seen = mm3(split(scores), solved[n, h])
        effective = queries[n] * grow[n, h] - seen[:, :DK]
        if n == 0:
            base[n, h], mapped[n, h] = seen[:, DK:], effective
        else:
            ahead = prefixes[n, h]
            if n == 3:
                ahead = compose(ahead[0], ahead[1])
            through = mm3(effective, ahead)
            base[n, h], mapped[n, h] = seen[:, DK:] + through[:, DK:], through[:, :DK]

    for h in range(2):
        along_x.finish(h)
        lower = compose(xs[1, h], xs[0, h])
        upper = compose(xs[3, h], xs[2, h])
        ys[y, h] = compose(upper, lower).astype(BF16)
        along_y.start(h)

    state = {}
    inside = {}
    start = jnp.where(
        lax.broadcasted_iota(jnp.int32, (DK, 2 * DK), 0)
        == lax.broadcasted_iota(jnp.int32, (DK, 2 * DK), 1),
        1.0,
        0.0,
    )
    for h in range(2):
        running = jnp.where(x > 0, xs[0, h].astype(F32), start)
        for other in range(1, 3):
            running = jnp.where(x > other, compose(xs[other, h], running), running)
        inside[h] = running
    gain = gain_ref[...]
    for h in range(2):
        along_y.finish(h)
        running = jnp.where(y > 0, ys[0, h, :, DK:].astype(F32), 0.0)
        for other in range(1, 3):
            after = mm2(ys[other, h, :, :DK], running) + ys[other, h, :, DK:].astype(F32)
            running = jnp.where(y > other, after, running)
        state[h] = split(mm3(inside[h][:, :DK], running) + inside[h][:, DK:])
        cols = slice(h * DV, (h + 1) * DV)
        for n in range(chunks):
            rows = slice(n * CH, (n + 1) * CH)
            readout = base[n, h] + mm3(mapped[n, h], state[h])
            scaled = readout * lax.rsqrt(jnp.mean(readout * readout, axis=-1, keepdims=True) + EPS)
            gate = g_ref[rows, cols].astype(F32)
            mixed = (scaled * gain * (gate / (1.0 + jnp.exp(-gate)))).astype(BF16)
            for i in range(4):
                at_chip = (2 * n + i // 2) * 32
                mix[i % 2, h, at_chip : at_chip + 32] = mixed[32 * i : 32 * i + 32]
        ready(h)

    def drain():
        along_x.drain()
        along_y.drain()

    return drain


class RingSum:
    def __init__(self, own, out, came, sem, ring):
        self.own, self.out, self.came, self.sem, self.ring = own, out, came, sem, ring
        self.sent = []

    def hop(self, way, step, part):
        return send_to(
            self.out.at[way, step, part],
            self.came.at[way, step, part],
            self.sem.at[0, way, step, part],
            self.sem.at[1, way, step, part],
            "exp",
            self.ring[way],
        )

    def launch(self, way, part):
        self.out[way, 0, part] = self.own[4, :, part * WIDE : (part + 1) * WIDE].astype(BF16)
        copy = self.hop(way, 0, part)
        copy.start()
        self.sent.append(copy)

    def run(self, prepare):
        for step in range(1, 4):
            prepare(step)
            for turn, way, part in turns():
                d = 4 - step if way == 0 else 4 + step
                total = self.own[d, :, part * WIDE : (part + 1) * WIDE]
                if step >= 2 or (step == 1 and turn == 0):
                    self.hop(way, step - 1, part).wait_recv()
                    total = total + self.came[way, step - 1, part].astype(F32)
                self.out[way, step, part] = total.astype(BF16)
                copy = self.hop(way, step, part)
                copy.start()
                self.sent.append(copy)
        prepare(4)

    def result(self, part):
        total = self.own[0, :, part * WIDE : (part + 1) * WIDE]
        for way in range(2):
            self.hop(way, 3, part).wait_recv()
            total = total + self.came[way, 3, part].astype(F32)
        return total

    def drain(self):
        for copy in self.sent:
            copy.wait_send()


def turns():
    some = PARTS // 2
    return [
        (turn, way, (way if turn == 0 else 1 - way) * some + i)
        for turn in range(2)
        for i in range(some)
        for way in range(2)
    ]


def kernel(*refs):
    inputs, o_ref, scratch = refs[:15], refs[15], refs[16:]
    held, scratch = scratch[:15], scratch[15:]
    (own, out, came, res, tokens, table, mix, mix_in, xs, ys) = scratch[:10]
    (wsem, csem, msem, tsem, rsem, gsem, *seq_sems) = scratch[10:]
    (hid_ref, q, k, v, g, ld, wr, gain, ow, post_ref, ids_ref, route_ref, gw, uw, dw) = held
    weights = (8, 12, 13, 14)

    place = lax.axis_index("exp")
    z, core = lax.div(place, 2), lax.rem(place, 2)
    chips = [lax.rem(z + d, 8) * 2 + core for d in range(8)]
    sibling = z * 2 + (1 - core)
    ring = (chips[1], chips[7])
    turn_at = lax.axis_index("seq")
    x, y = lax.rem(turn_at, 4), lax.div(turn_at, 4)
    x_peers = [y * 4 + lax.rem(x + d, 4) for d in range(4)]
    y_peers = [lax.rem(y + d, 4) * 4 + x for d in range(4)]
    at = (x, y, x_peers, y_peers)
    meet = greet(
        [("seq", peer) for peer in x_peers[1:] + y_peers[1:]]
        + [("exp", peer) for peer in chips[1:] + [sibling]]
    )

    loads, shared = [], []
    for i, (src, dst) in enumerate(zip(inputs, held)):
        if i in weights:
            flat = src if i == 8 else src.at[0]
            n = weights.index(i)
            shared.append(
                send_to(flat, dst.at[core], csem.at[0, n], csem.at[1, n], "exp", sibling)
            )
            dst, src = dst.at[core], flat
        loads.append(pltpu.make_async_copy(src, dst, wsem.at[i]))
    arriving = [
        send_to(
            held[i].at[1 - core], held[i].at[1 - core], csem.at[0, n], csem.at[1, n], "exp", sibling
        )
        for n, i in enumerate(weights)
    ]
    early, middle = (2, 1, 5, 6, 3), (10, 11, 4, 7, 0, 9)
    for i in early + middle:
        loads[i].start()
    for i in early:
        loads[i].wait()
    for i in weights:
        loads[i].start()

    lane = lax.broadcasted_iota(jnp.int32, (32, 128), 1).astype(F32)
    sent = []

    def begin(copy):
        copy.start()
        sent.append(copy)

    def late():
        for copy in shared:
            copy.start()
        for i in middle:
            loads[i].wait()
        ids = ids_ref[...].astype(F32)
        routes = route_ref[...].astype(F32)
        same = lax.broadcasted_iota(jnp.int32, (32, 32), 0) == lax.broadcasted_iota(
            jnp.int32, (32, 32), 1
        )
        shares = jnp.zeros((32, 128), F32)
        for j in range(4):
            named, share = (
                jnp.sum(jnp.where(same, a[j : j + 1, :], 0.0), axis=1, keepdims=True)
                for a in (ids, routes)
            )
            shares = shares + jnp.where(lane == named, share, 0.0)
        table[0] = shares.astype(BF16)
        for d in range(1, 8):
            begin(share_table(d))

    def share_table(d):
        return send_to(
            table.at[0], table.at[8 - d], tsem.at[0, 8 - d], tsem.at[1, 8 - d], "exp", chips[d]
        )

    def mix_copy(h):
        return send_to(
            mix.at[1 - core, h], mix_in.at[h], msem.at[0, h], msem.at[1, h], "exp", sibling
        )

    drain_seq = seq_part(
        q,
        k,
        v,
        g,
        ld,
        wr,
        gain,
        mix,
        xs,
        ys,
        seq_sems,
        at,
        meet,
        late,
        lambda h: begin(mix_copy(h)),
    )

    loads[8].wait()
    arriving[0].wait_recv()
    for h in range(2):
        mix_copy(h).wait_recv()

    def project(offsets):
        rows = [pl.ds(pl.multiple_of(lax.rem(z + d, 8) * 32, 32), 32) for d in offsets]
        mine, other = (
            jnp.concatenate(
                [jnp.concatenate([ref[h, r] for h in range(2)], axis=1) for r in rows], axis=0
            )
            for ref in (mix.at[core], mix_in)
        )
        block = mm(mine, ow[core]) + mm(other, ow[1 - core])
        for i, d in enumerate(offsets):
            own[0, d] = block[32 * i : 32 * i + 32]

    first = RingSum(own.at[0], out.at[0], came.at[0], rsem.at[0], ring)
    project((4,))
    for turn, way, part in turns():
        if turn == 0:
            first.launch(way, part)
    first.run(lambda step: project(((4,), (3, 5), (2, 6), (1, 7), (0,))[step]))
    for part in range(PARTS):
        cols = slice(part * WIDE, (part + 1) * WIDE)
        res[:, cols] = hid_ref[:, cols].astype(F32) + first.result(part)

    residual = res[...]
    normed = (
        residual
        * lax.rsqrt(jnp.mean(residual * residual, axis=-1, keepdims=True) + EPS)
        * post_ref[...]
    ).astype(BF16)
    for part in range(PARTS):
        tokens[0, part] = normed[:, part * WIDE : (part + 1) * WIDE]

    def onward(way, step, part):
        src = (8 - step) % 8 if way == 0 else step
        dst = 7 - step if way == 0 else step + 1
        return send_to(
            tokens.at[src, part],
            tokens.at[dst, part],
            gsem.at[0, way, step, part],
            gsem.at[1, way, step, part],
            "exp",
            ring[way],
        )

    def expert(offsets):
        picked = jnp.concatenate(
            [
                jnp.concatenate([tokens[d, part] for part in range(PARTS)], axis=1)
                for d in offsets
            ],
            axis=0,
        )
        for d in offsets:
            if d > 0:
                share_table(8 - d).wait_recv()
        shares = jnp.concatenate([table[d] for d in offsets], axis=0).astype(F32)
        lanes = lax.broadcasted_iota(jnp.int32, shares.shape, 1)
        hidden, share = [], []
        for e in range(2):
            gate = mm(picked, gw[e])
            up = mm(picked, uw[e])
            hidden.append((gate / (1.0 + jnp.exp(-gate)) * up).astype(BF16))
            share.append(
                jnp.sum(jnp.where(lanes == z * 2 + e, shares, 0.0), axis=1, keepdims=True)
            )

        def down(part):
            cols = slice(part * WIDE, (part + 1) * WIDE)
            total = sum(
                mm(hidden[e], dw[e, :, cols]).astype(BF16).astype(F32) * share[e]
                for e in range(2)
            )
            for i, d in enumerate(offsets):
                own[1, d, :, cols] = total[32 * i : 32 * i + 32]

        return down

    def expert_all(offsets):
        down = expert(offsets)
        for part in range(PARTS):
            down(part)

    for turn, way, part in turns():
        begin(onward(way, 0, part))
    for i in weights[1:]:
        loads[i].wait()
    for copy in arriving[1:]:
        copy.wait_recv()
    for step in range(1, 4):
        for turn, way, part in turns():
            onward(way, step - 1, part).wait_recv()
            if step < 3 or turn == 0:
                begin(onward(way, step, part))
        if step == 1:
            expert_all((0, 1, 7))
        elif step == 2:
            expert_all((2, 6))
    for turn, way, part in turns():
        if turn == 0:
            onward(way, 3, part).wait_recv()
    second = RingSum(own.at[1], out.at[1], came.at[1], rsem.at[1], ring)
    down = expert((3, 4, 5))
    for turn, way, part in turns():
        if turn == 0:
            down(part)
            second.launch(way, part)
    second.run(lambda step: None)
    for part in range(PARTS):
        cols = slice(part * WIDE, (part + 1) * WIDE)
        o_ref[:, cols] = (res[:, cols] + second.result(part)).astype(BF16)
    for copy in sent + shared:
        copy.wait_send()
    first.drain()
    second.drain()
    drain_seq()


def per_device(*args):
    args = list(args)
    args[7] = args[7].reshape(1, DV)
    args[9] = args[9].reshape(1, D)
    args[10] = args[10].T
    args[11] = args[11].T
    slots = pltpu.VMEM((4, 2, DK, 2 * DK), BF16)
    both = {8: (2,) + args[8].shape}
    for i in (12, 13, 14):
        both[i] = (2,) + args[i].shape[1:]
    scratch = [pltpu.VMEM(both.get(i, a.shape), a.dtype) for i, a in enumerate(args)] + [
        pltpu.VMEM((2, 8, 32, D), F32),
        pltpu.VMEM((2, 2, 4, PARTS, 32, WIDE), BF16),
        pltpu.VMEM((2, 2, 4, PARTS, 32, WIDE), BF16),
        pltpu.VMEM((32, D), F32),
        pltpu.VMEM((8, PARTS, 32, WIDE), BF16),
        pltpu.VMEM((8, 32, 128), BF16),
        pltpu.VMEM((2, 2, 256, DV), BF16),
        pltpu.VMEM((2, 256, DV), BF16),
        slots,
        slots,
        pltpu.SemaphoreType.DMA((15,)),
        pltpu.SemaphoreType.DMA((2, 4)),
        pltpu.SemaphoreType.DMA((2, 2)),
        pltpu.SemaphoreType.DMA((2, 8)),
        pltpu.SemaphoreType.DMA((2, 2, 2, 4, PARTS)),
        pltpu.SemaphoreType.DMA((2, 2, 4, PARTS)),
    ]
    return pl.pallas_call(
        kernel,
        out_shape=jax.ShapeDtypeStruct(args[0].shape, BF16),
        in_specs=[pl.BlockSpec(memory_space=pl.ANY)] * 15,
        out_specs=pl.BlockSpec(memory_space=pltpu.VMEM),
        scratch_shapes=scratch + [pltpu.SemaphoreType.DMA((4, 4))] * 4,
        compiler_params=pltpu.CompilerParams(
            collective_id=0, has_side_effects=True, vmem_limit_bytes=62 * 1024 * 1024
        ),
        name="layer",
    )(*args)


def solution(mesh):
    in_specs = (
        P(("seq", "exp"), None),
        P("seq", "exp"),
        P("seq", "exp"),
        P("seq", "exp"),
        P("seq", "exp"),
        P("exp", "seq"),
        P("exp", "seq"),
        P(),
        P("exp", None),
        P(),
        P(("seq", "exp"), None),
        P(("seq", "exp"), None),
        P("exp", None, None),
        P("exp", None, None),
        P("exp", None, None),
    )
    out_specs = P(("seq", "exp"), None)
    return jax.shard_map(
        per_device, mesh=mesh, in_specs=in_specs, out_specs=out_specs, check_vma=False
    )
```

```python
import functools

import jax
import jax.numpy as jnp
from jax import lax
from jax.experimental import pallas as pl
from jax.experimental.pallas import tpu as pltpu
from jax.sharding import PartitionSpec as P

D = 2048
FF = 512
DK = 128
DV = 128
EPS = 1e-06
CH = 128
PARTS = 4
WIDE = D // PARTS
F32 = jnp.float32
BF16 = jnp.bfloat16
MESH = pl.DeviceIdType.MESH
NN = (((1,), (0,)), ((), ()))
NT = (((1,), (1,)), ((), ()))
TN = (((0,), (0,)), ((), ()))


def mm(a, b, dims=NN):
    return lax.dot_general(a, b, dims, preferred_element_type=F32)


def split(a):
    hi = a.astype(BF16)
    return hi, (a - hi.astype(F32)).astype(BF16)


def mm3(a, b, dims=NN):
    ah, al = a if isinstance(a, tuple) else split(a)
    bh, bl = b if isinstance(b, tuple) else split(b)
    if dims != NN:
        return mm(ah, bh, dims) + (mm(ah, bl, dims) + mm(al, bh, dims))
    n = bh.shape[1]
    left = jnp.concatenate([ah, al], axis=1)
    if n > 128:
        return mm(left, jnp.concatenate([bh, bh], axis=0)) + mm(ah, bl)
    right = jnp.concatenate(
        [
            jnp.concatenate([bh, bl], axis=1),
            jnp.concatenate([bh, jnp.zeros_like(bl)], axis=1),
        ],
        axis=0,
    )
    both = mm(left, right)
    return both[:, :n] + both[:, n:]


def mm2(a, b, dims=NN):
    bh, bl = split(b)
    return mm(a, bh, dims) + mm(a, bl, dims)


def greet(peers):
    barrier = pltpu.get_barrier_semaphore()
    for axis, peer in peers:
        pl.semaphore_signal(barrier, inc=1, device_id={axis: peer}, device_id_type=MESH)
    return lambda: pl.semaphore_wait(barrier, len(peers))


def send_to(src, dst, send_sem, recv_sem, axis, peer):
    return pltpu.make_async_remote_copy(
        src_ref=src,
        dst_ref=dst,
        send_sem=send_sem,
        recv_sem=recv_sem,
        device_id={axis: peer},
        device_id_type=MESH,
    )


class Gather4:
    def __init__(self, slots, me, peers, ssem, rsem):
        self.slots, self.me, self.peers, self.ssem, self.rsem = slots, me, peers, ssem, rsem
        self.sent = []

    def copy(self, d, h, i):
        place = lax.rem(self.me + d, 4)
        piece = self.slots.at[place, h, pl.ds(i * 64, 64)]
        return piece, h * 2 + i

    def start(self, h):
        for i in range(2):
            piece, at = self.copy(0, h, i)
            for d in (2, 1, 3):
                copy = send_to(
                    piece, piece, self.ssem.at[d, at], self.rsem.at[d, at], "seq", self.peers[d]
                )
                copy.start()
                self.sent.append(copy)

    def finish(self, h):
        for d in (1, 3, 2):
            for i in range(2):
                piece, at = self.copy(4 - d, h, i)
                send_to(
                    piece, piece, self.ssem.at[d, at], self.rsem.at[d, at], "seq", self.peers[d]
                ).wait_recv()

    def drain(self):
        for copy in self.sent:
            copy.wait_send()


def compose(later, earlier):
    later = later.astype(F32)
    earlier = earlier.astype(F32)
    joined = mm3(later[:, :DK], earlier)
    return joined + jnp.concatenate([jnp.zeros((DK, DK), F32), later[:, DK:]], axis=1)


def seq_part(q_ref, k_ref, v_ref, g_ref, ld_ref, wr_ref, gain_ref, mix, xs, ys, sems, at, need, meet, late, ready):
    xsend, xrecv, ysend, yrecv = sems
    x, y, x_peers, y_peers = at
    chunks = q_ref.shape[0] // CH
    row = lax.broadcasted_iota(jnp.int32, (CH, CH), 0)
    col = lax.broadcasted_iota(jnp.int32, (CH, CH), 1)
    eye = row == col
    causal = row >= col
    strict = row > col
    pairs = [(n, h) for n in range(chunks) for h in range(2)]

    keys, kk, qk, queries = [], [], [], []
    need(2)
    for n in range(chunks):
        rows = slice(n * CH, (n + 1) * CH)
        k = k_ref[rows, :].astype(F32)
        k = k * lax.rsqrt(jnp.sum(k * k, axis=-1, keepdims=True) + EPS)
        ks = split(k)
        keys.append(k)
        kk.append(mm3(ks, ks, NT))

    decay, grow, tail, end, strict_part, rate = {}, {}, {}, {}, {}, {}
    step, solved, prefixes = {}, {}, {}
    along_x = Gather4(xs, x, x_peers, xsend, xrecv)
    along_y = Gather4(ys, y, y_peers, ysend, yrecv)
    need(5, 6)
    for h in range(2):
        mine = [(n, h) for n in range(chunks)]
        for n, h in mine:
            ld_row = ld_ref[h : h + 1, n * CH : (n + 1) * CH]
            ld_all = jnp.broadcast_to(ld_row, (CH, CH))
            wr_all = jnp.broadcast_to(wr_ref[h : h + 1, n * CH : (n + 1) * CH], (CH, CH))
            ld_col = jnp.sum(jnp.where(eye, ld_all, 0.0), axis=1, keepdims=True)
            cum_col = jnp.sum(jnp.where(causal, ld_all, 0.0), axis=1, keepdims=True)
            cum_row = jnp.sum(jnp.where(row <= col, ld_col, 0.0), axis=0, keepdims=True)
            rate[n, h] = jnp.sum(jnp.where(eye, wr_all, 0.0), axis=1, keepdims=True)
            total = jnp.sum(ld_row, axis=1, keepdims=True)
            decay[n, h] = jnp.where(causal, jnp.exp(jnp.where(causal, cum_col - cum_row, 0.0)), 0.0)
            grow[n, h] = jnp.exp(cum_col)
            tail[n, h] = jnp.exp(total - cum_col)
            end[n, h] = jnp.exp(total)
            strict_part[n, h] = jnp.where(strict, kk[n] * decay[n, h] * rate[n, h], 0.0)

        inverse = {}
        for p in mine:
            low = jnp.where((row // 2 == col // 2) & strict, strict_part[p], 0.0)
            inverse[p] = jnp.where(eye, 1.0, -low)
        width = 2
        while width < CH:
            mask = (row // (2 * width) == col // (2 * width)) & (row // width > col // width)
            inner = {}
            held = {}
            for p in mine:
                held[p] = split(inverse[p])
                inner[p] = mm3(split(jnp.where(mask, strict_part[p], 0.0)), held[p])
            for p in mine:
                inverse[p] = inverse[p] - mm3(held[p], split(inner[p]))
            width *= 2

        if h == 0:
            need(3)
        for n, h in mine:
            value = v_ref[n * CH : (n + 1) * CH, h * DV : (h + 1) * DV].astype(F32)
            sides = jnp.concatenate([keys[n] * (rate[n, h] * grow[n, h]), value * rate[n, h]], axis=1)
            solved[n, h] = split(mm3(inverse[n, h], sides))
        for n, h in mine:
            fed = mm3(split(keys[n] * tail[n, h]), solved[n, h], TN)
            step[n, h] = jnp.concatenate(
                [jnp.where(eye, end[n, h], 0.0) - fed[:, :DK], fed[:, DK:]], axis=1
            )
        first = compose(step[1, h], step[0, h])
        second = compose(step[3, h], step[2, h])
        whole = compose(second, first)
        xs[x, h] = whole.astype(BF16)
        if h == 0:
            meet()
        along_x.start(h)
        prefixes[1, h] = step[0, h]
        prefixes[2, h] = first
        prefixes[3, h] = (step[2, h], first)
    late()

    base, mapped = {}, {}
    need(1)
    for n in range(chunks):
        q = q_ref[n * CH : (n + 1) * CH, :].astype(F32)
        q = q * lax.rsqrt(jnp.sum(q * q, axis=-1, keepdims=True) + EPS) * DK ** (-0.5)
        queries.append(q)
        qk.append(mm3(split(q), split(keys[n]), NT))
    for n, h in pairs:
        scores = qk[n] * decay[n, h]
        seen = mm3(split(scores), solved[n, h])
        effective = queries[n] * grow[n, h] - seen[:, :DK]
        if n == 0:
            base[n, h], mapped[n, h] = seen[:, DK:], effective
        else:
            ahead = prefixes[n, h]
            if n == 3:
                ahead = compose(ahead[0], ahead[1])
            through = mm3(effective, ahead)
            base[n, h], mapped[n, h] = seen[:, DK:] + through[:, DK:], through[:, :DK]

    for h in range(2):
        along_x.finish(h)
        lower = compose(xs[1, h], xs[0, h])
        upper = compose(xs[3, h], xs[2, h])
        ys[y, h] = compose(upper, lower).astype(BF16)
        along_y.start(h)

    state = {}
    inside = {}
    start = jnp.where(
        lax.broadcasted_iota(jnp.int32, (DK, 2 * DK), 0)
        == lax.broadcasted_iota(jnp.int32, (DK, 2 * DK), 1),
        1.0,
        0.0,
    )
    for h in range(2):
        running = jnp.where(x > 0, xs[0, h].astype(F32), start)
        for other in range(1, 3):
            running = jnp.where(x > other, compose(xs[other, h], running), running)
        inside[h] = running
    gain = gain_ref[...]
    for h in range(2):
        along_y.finish(h)
        running = jnp.where(y > 0, ys[0, h, :, DK:].astype(F32), 0.0)
        for other in range(1, 3):
            after = mm2(ys[other, h, :, :DK], running) + ys[other, h, :, DK:].astype(F32)
            running = jnp.where(y > other, after, running)
        state[h] = split(mm3(inside[h][:, :DK], running) + inside[h][:, DK:])
        cols = slice(h * DV, (h + 1) * DV)
        for n in range(chunks):
            rows = slice(n * CH, (n + 1) * CH)
            readout = base[n, h] + mm3(mapped[n, h], state[h])
            scaled = readout * lax.rsqrt(jnp.mean(readout * readout, axis=-1, keepdims=True) + EPS)
            gate = g_ref[rows, cols].astype(F32)
            mixed = (scaled * gain * (gate / (1.0 + jnp.exp(-gate)))).astype(BF16)
            for i in range(4):
                at_chip = (2 * n + i // 2) * 32
                mix[i % 2, h, at_chip : at_chip + 32] = mixed[32 * i : 32 * i + 32]
        ready(h)

    def drain():
        along_x.drain()
        along_y.drain()

    return drain


class RingSum:
    def __init__(self, own, out, came, sem, ring):
        self.own, self.out, self.came, self.sem, self.ring = own, out, came, sem, ring
        self.sent = []

    def hop(self, way, step, part):
        return send_to(
            self.out.at[way, step, part],
            self.came.at[way, step, part],
            self.sem.at[0, way, step, part],
            self.sem.at[1, way, step, part],
            "exp",
            self.ring[way],
        )

    def launch(self, way, part):
        self.out[way, 0, part] = self.own[4, :, part * WIDE : (part + 1) * WIDE].astype(BF16)
        copy = self.hop(way, 0, part)
        copy.start()
        self.sent.append(copy)

    def run(self, prepare):
        for step in range(1, 4):
            prepare(step)
            for turn, way, part in turns()[2 * (PARTS // 2) :] + turns()[: 2 * (PARTS // 2)]:
                d = 4 - step if way == 0 else 4 + step
                total = self.own[d, :, part * WIDE : (part + 1) * WIDE]
                if step >= 2 or (step == 1 and turn == 0):
                    self.hop(way, step - 1, part).wait_recv()
                    total = total + self.came[way, step - 1, part].astype(F32)
                self.out[way, step, part] = total.astype(BF16)
                copy = self.hop(way, step, part)
                copy.start()
                self.sent.append(copy)
        prepare(4)

    def result(self, part):
        total = self.own[0, :, part * WIDE : (part + 1) * WIDE]
        for way in range(2):
            self.hop(way, 3, part).wait_recv()
            total = total + self.came[way, 3, part].astype(F32)
        return total

    def drain(self):
        for copy in self.sent:
            copy.wait_send()


def turns():
    some = PARTS // 2
    return [
        (turn, way, (way if turn == 0 else 1 - way) * some + i)
        for turn in range(2)
        for i in range(some)
        for way in range(2)
    ]


def kernel(*refs):
    inputs, o_ref, scratch = refs[:15], refs[15], refs[16:]
    held, scratch = scratch[:15], scratch[15:]
    (own, out, came, res, tokens, normed, table, mix, mix_in, xs, ys) = scratch[:11]
    (wsem, csem, msem, tsem, rsem, gsem, *seq_sems) = scratch[11:]
    (hid_ref, q, k, v, g, ld, wr, gain, ow, post_ref, ids_ref, route_ref, gw, uw, dw) = held
    weights = (8, 12, 13, 14)

    place = lax.axis_index("exp")
    z, core = lax.div(place, 2), lax.rem(place, 2)
    chips = [lax.rem(z + d, 8) * 2 + core for d in range(8)]
    sibling = z * 2 + (1 - core)
    ring = (chips[1], chips[7])
    turn_at = lax.axis_index("seq")
    x, y = lax.rem(turn_at, 4), lax.div(turn_at, 4)
    x_peers = [y * 4 + lax.rem(x + d, 4) for d in range(4)]
    y_peers = [lax.rem(y + d, 4) * 4 + x for d in range(4)]
    at = (x, y, x_peers, y_peers)
    meet = greet(
        [("seq", peer) for peer in x_peers[1:] + y_peers[1:]]
        + [("exp", peer) for peer in chips[1:] + [sibling]]
    )

    loads, shared = [], []
    for i, (src, dst) in enumerate(zip(inputs, held)):
        if i in weights:
            flat = src if i == 8 else src.at[0]
            n = weights.index(i)
            shared.append(
                send_to(flat, dst.at[core], csem.at[0, n], csem.at[1, n], "exp", sibling)
            )
            dst, src = dst.at[core], flat
        loads.append(pltpu.make_async_copy(src, dst, wsem.at[i]))
    arriving = [
        send_to(
            held[i].at[1 - core], held[i].at[1 - core], csem.at[0, n], csem.at[1, n], "exp", sibling
        )
        for n, i in enumerate(weights)
    ]
    early, middle = (2, 5, 6, 3, 1), (10, 11, 4, 7, 0, 9)
    for i in early + middle:
        loads[i].start()

    def need(*which):
        for i in which:
            loads[i].wait()

    lane = lax.broadcasted_iota(jnp.int32, (32, 128), 1).astype(F32)
    sent = []

    def begin(copy):
        copy.start()
        sent.append(copy)

    def late():
        for i, copy in zip(weights, shared):
            loads[i].start()
            copy.start()
        for i in middle:
            loads[i].wait()
        ids = ids_ref[...].astype(F32)
        routes = route_ref[...].astype(F32)
        same = lax.broadcasted_iota(jnp.int32, (32, 32), 0) == lax.broadcasted_iota(
            jnp.int32, (32, 32), 1
        )
        shares = jnp.zeros((32, 128), F32)
        for j in range(4):
            named, share = (
                jnp.sum(jnp.where(same, a[j : j + 1, :], 0.0), axis=1, keepdims=True)
                for a in (ids, routes)
            )
            shares = shares + jnp.where(lane == named, share, 0.0)
        table[0] = shares.astype(BF16)
        for d in range(1, 8):
            begin(share_table(d))

    def share_table(d):
        return send_to(
            table.at[0], table.at[8 - d], tsem.at[0, 8 - d], tsem.at[1, 8 - d], "exp", chips[d]
        )

    def mix_copy(h):
        return send_to(
            mix.at[1 - core, h], mix_in.at[h], msem.at[0, h], msem.at[1, h], "exp", sibling
        )

    drain_seq = seq_part(
        q,
        k,
        v,
        g,
        ld,
        wr,
        gain,
        mix,
        xs,
        ys,
        seq_sems,
        at,
        need,
        meet,
        late,
        lambda h: begin(mix_copy(h)),
    )

    def mixed_rows(ref, offsets):
        rows = [pl.ds(pl.multiple_of(lax.rem(z + d, 8) * 32, 32), 32) for d in offsets]
        return jnp.concatenate(
            [jnp.concatenate([ref[h, r] for h in range(2)], axis=1) for r in rows], axis=0
        )

    def project(offsets):
        block = mm(mixed_rows(mix_in, offsets), ow[1 - core])
        for i, d in enumerate(offsets):
            own[0, d] = own[0, d] + block[32 * i : 32 * i + 32]

    loads[8].wait()
    block = mm(mixed_rows(mix.at[core], range(8)), ow[core])
    for d in range(8):
        own[0, d] = block[32 * d : 32 * d + 32]
    arriving[0].wait_recv()
    for h in range(2):
        mix_copy(h).wait_recv()
    first = RingSum(own.at[0], out.at[0], came.at[0], rsem.at[0], ring)
    project((4,))
    for turn, way, part in turns():
        if turn == 0:
            first.launch(way, part)
    first.run(lambda step: project(((4,), (3, 5), (2, 6), (1, 7), (0,))[step]))
    def onward(way, step, part):
        src = (8 - step) % 8 if way == 0 else step
        dst = 7 - step if way == 0 else step + 1
        return send_to(
            tokens.at[src, part],
            tokens.at[dst, part],
            gsem.at[0, way, step, part],
            gsem.at[1, way, step, part],
            "exp",
            ring[way],
        )

    def settle(offsets):
        for d in offsets:
            row = jnp.concatenate([tokens[d, part] for part in range(PARTS)], axis=1).astype(F32)
            scale = lax.rsqrt(jnp.mean(row * row, axis=-1, keepdims=True) + EPS)
            normed[d] = (row * scale * post_ref[...]).astype(BF16)

    def expert(offsets):
        for d in offsets:
            if d > 0:
                share_table(8 - d).wait_recv()
        shares = jnp.concatenate([table[d] for d in offsets], axis=0).astype(F32)
        lanes = lax.broadcasted_iota(jnp.int32, shares.shape, 1)
        hidden, share = [], []

        def close(e, gate, up):
            hidden.append((gate / (1.0 + jnp.exp(-gate)) * up).astype(BF16))
            share.append(
                jnp.sum(jnp.where(lanes == z * 2 + e, shares, 0.0), axis=1, keepdims=True)
            )

        def widen(e):
            picked = jnp.concatenate([normed[d] for d in offsets], axis=0)
            close(e, mm(picked, gw[e]), mm(picked, uw[e]))

        def widen_late():
            sums = [[0.0, 0.0], [0.0, 0.0]]
            square = 0.0
            for i in range(PARTS // 2):
                for way in range(2):
                    onward(way, 3, way * (PARTS // 2) + i).wait_recv()
                for part in (i, PARTS // 2 + i):
                    cols = slice(part * WIDE, (part + 1) * WIDE)
                    row = jnp.concatenate([tokens[d, part] for d in offsets], axis=0).astype(F32)
                    square = square + jnp.sum(row * row, axis=-1, keepdims=True)
                    row = (row * post_ref[:, cols]).astype(BF16)
                    for e in range(2):
                        for k, w in enumerate((gw, uw)):
                            sums[e][k] = sums[e][k] + mm(row, w[e, cols, :])
            scale = lax.rsqrt(square * (1.0 / D) + EPS)
            for e in range(2):
                close(e, sums[e][0] * scale, sums[e][1] * scale)

        def down(part):
            cols = slice(part * WIDE, (part + 1) * WIDE)
            total = sum(
                mm(hidden[e], dw[e, :, cols]).astype(BF16).astype(F32) * share[e]
                for e in range(2)
            )
            for i, d in enumerate(offsets):
                own[1, d, :, cols] = total[32 * i : 32 * i + 32]

        return widen, widen_late, down

    for part in (i + j for i in range(PARTS // 2) for j in (0, PARTS // 2)):
        cols = slice(part * WIDE, (part + 1) * WIDE)
        block = hid_ref[:, cols].astype(F32) + first.result(part)
        res[:, cols] = block
        tokens[0, part] = block.astype(BF16)
        ahead = 0 if part < PARTS // 2 else 1
        for way in (ahead, 1 - ahead):
            begin(onward(way, 0, part))
    settle((0,))
    for i in weights[1:]:
        loads[i].wait()
    for copy in arriving[1:]:
        copy.wait_recv()

    def pass_on(step):
        for turn, way, part in turns():
            onward(way, step - 1, part).wait_recv()
            if step < 3 or turn == 0:
                begin(onward(way, step, part))
        if step < 3:
            settle((8 - step, step))

    pass_on(1)
    near_widen, _, near_down = expert((0, 1, 7))
    near_widen(0)
    near_widen(1)
    pass_on(2)
    for part in range(PARTS):
        near_down(part)
    next_widen, _, next_down = expert((2, 6))
    next_widen(0)
    pass_on(3)
    next_widen(1)
    for part in range(PARTS):
        next_down(part)
    second = RingSum(own.at[1], out.at[1], came.at[1], rsem.at[1], ring)
    _, widen_late, down = expert((3, 4, 5))
    widen_late()
    for turn, way, part in turns():
        if turn == 0:
            down(part)
            second.launch(way, part)
    second.run(lambda step: None)
    for part in (i + j for i in range(PARTS // 2) for j in (0, PARTS // 2)):
        cols = slice(part * WIDE, (part + 1) * WIDE)
        o_ref[:, cols] = (res[:, cols] + second.result(part)).astype(BF16)
    for copy in sent + shared:
        copy.wait_send()
    first.drain()
    second.drain()
    drain_seq()


def per_device(*args):
    args = list(args)
    args[7] = args[7].reshape(1, DV)
    args[9] = args[9].reshape(1, D)
    args[10] = args[10].T
    args[11] = args[11].T
    slots = pltpu.VMEM((4, 2, DK, 2 * DK), BF16)
    both = {8: (2,) + args[8].shape}
    for i in (12, 13, 14):
        both[i] = (2,) + args[i].shape[1:]
    scratch = [pltpu.VMEM(both.get(i, a.shape), a.dtype) for i, a in enumerate(args)] + [
        pltpu.VMEM((2, 8, 32, D), F32),
        pltpu.VMEM((2, 2, 4, PARTS, 32, WIDE), BF16),
        pltpu.VMEM((2, 2, 4, PARTS, 32, WIDE), BF16),
        pltpu.VMEM((32, D), F32),
        pltpu.VMEM((8, PARTS, 32, WIDE), BF16),
        pltpu.VMEM((8, 32, D), BF16),
        pltpu.VMEM((8, 32, 128), BF16),
        pltpu.VMEM((2, 2, 256, DV), BF16),
        pltpu.VMEM((2, 256, DV), BF16),
        slots,
        slots,
        pltpu.SemaphoreType.DMA((15,)),
        pltpu.SemaphoreType.DMA((2, 4)),
        pltpu.SemaphoreType.DMA((2, 2)),
        pltpu.SemaphoreType.DMA((2, 8)),
        pltpu.SemaphoreType.DMA((2, 2, 2, 4, PARTS)),
        pltpu.SemaphoreType.DMA((2, 2, 4, PARTS)),
    ]
    return pl.pallas_call(
        kernel,
        out_shape=jax.ShapeDtypeStruct(args[0].shape, BF16),
        in_specs=[pl.BlockSpec(memory_space=pl.ANY)] * 15,
        out_specs=pl.BlockSpec(memory_space=pltpu.VMEM),
        scratch_shapes=scratch + [pltpu.SemaphoreType.DMA((4, 4))] * 4,
        compiler_params=pltpu.CompilerParams(
            collective_id=0, has_side_effects=True, vmem_limit_bytes=62 * 1024 * 1024
        ),
        name="layer",
    )(*args)


def solution(mesh):
    in_specs = (
        P(("seq", "exp"), None),
        P("seq", "exp"),
        P("seq", "exp"),
        P("seq", "exp"),
        P("seq", "exp"),
        P("exp", "seq"),
        P("exp", "seq"),
        P(),
        P("exp", None),
        P(),
        P(("seq", "exp"), None),
        P(("seq", "exp"), None),
        P("exp", None, None),
        P("exp", None, None),
        P("exp", None, None),
    )
    out_specs = P(("seq", "exp"), None)
    return jax.shard_map(
        per_device, mesh=mesh, in_specs=in_specs, out_specs=out_specs, check_vma=False
    )
```

```python
import functools

import jax
import jax.numpy as jnp
from jax import lax
from jax.experimental import pallas as pl
from jax.experimental.pallas import tpu as pltpu
from jax.sharding import PartitionSpec as P

D = 2048
FF = 512
DK = 128
DV = 128
EPS = 1e-06
CH = 128
PARTS = 4
WIDE = D // PARTS
F32 = jnp.float32
BF16 = jnp.bfloat16
MESH = pl.DeviceIdType.MESH
NN = (((1,), (0,)), ((), ()))
NT = (((1,), (1,)), ((), ()))
TN = (((0,), (0,)), ((), ()))


def mm(a, b, dims=NN):
    return lax.dot_general(a, b, dims, preferred_element_type=F32)


def split(a):
    hi = a.astype(BF16)
    return hi, (a - hi.astype(F32)).astype(BF16)


def mm3(a, b, dims=NN):
    ah, al = a if isinstance(a, tuple) else split(a)
    bh, bl = b if isinstance(b, tuple) else split(b)
    if dims != NN:
        return mm(ah, bh, dims) + (mm(ah, bl, dims) + mm(al, bh, dims))
    n = bh.shape[1]
    left = jnp.concatenate([ah, al], axis=1)
    if n > 128:
        return mm(left, jnp.concatenate([bh, bh], axis=0)) + mm(ah, bl)
    right = jnp.concatenate(
        [
            jnp.concatenate([bh, bl], axis=1),
            jnp.concatenate([bh, jnp.zeros_like(bl)], axis=1),
        ],
        axis=0,
    )
    both = mm(left, right)
    return both[:, :n] + both[:, n:]


def mm2(a, b, dims=NN):
    bh, bl = split(b)
    return mm(a, bh, dims) + mm(a, bl, dims)


def greet(peers):
    barrier = pltpu.get_barrier_semaphore()
    for axis, peer in peers:
        pl.semaphore_signal(barrier, inc=1, device_id={axis: peer}, device_id_type=MESH)
    return lambda: pl.semaphore_wait(barrier, len(peers))


def send_to(src, dst, send_sem, recv_sem, axis, peer):
    return pltpu.make_async_remote_copy(
        src_ref=src,
        dst_ref=dst,
        send_sem=send_sem,
        recv_sem=recv_sem,
        device_id={axis: peer},
        device_id_type=MESH,
    )


class Gather4:
    def __init__(self, slots, me, peers, ssem, rsem, upward=False):
        self.slots, self.me, self.peers, self.ssem, self.rsem = slots, me, peers, ssem, rsem
        self.upward = upward
        self.sent = []

    def copy(self, d, h, i):
        place = lax.rem(self.me + d, 4)
        piece = self.slots.at[place, h, pl.ds(i * 64, 64)]
        return piece, h * 2 + i

    def start(self, h):
        for i in range(2):
            piece, at = self.copy(0, h, i)
            for d in (2, 1, 3):
                copy = send_to(
                    piece, piece, self.ssem.at[d, at], self.rsem.at[d, at], "seq", self.peers[d]
                )
                self.when(self.me + d < 4, copy.start)
                self.sent.append((d, copy))

    def when(self, holds, act):
        if self.upward:
            pl.when(holds)(act)
        else:
            act()

    def finish(self, h):
        for d in (1, 3, 2):
            for i in range(2):
                piece, at = self.copy(4 - d, h, i)
                came = send_to(
                    piece, piece, self.ssem.at[d, at], self.rsem.at[d, at], "seq", self.peers[d]
                )
                self.when(self.me >= d, came.wait_recv)

    def drain(self):
        for d, copy in self.sent:
            self.when(self.me + d < 4, copy.wait_send)


def compose(later, earlier):
    later = later.astype(F32)
    earlier = earlier.astype(F32)
    joined = mm3(later[:, :DK], earlier)
    return joined + jnp.concatenate([jnp.zeros((DK, DK), F32), later[:, DK:]], axis=1)


def seq_part(q_ref, k_ref, v_ref, g_ref, ld_ref, wr_ref, gain_ref, mix, xs, ys, sems, at, need, meet, late, ready):
    xsend, xrecv, ysend, yrecv = sems
    x, y, x_peers, y_peers = at
    chunks = q_ref.shape[0] // CH
    row = lax.broadcasted_iota(jnp.int32, (CH, CH), 0)
    col = lax.broadcasted_iota(jnp.int32, (CH, CH), 1)
    eye = row == col
    causal = row >= col
    strict = row > col
    pairs = [(n, h) for n in range(chunks) for h in range(2)]

    keys, kk, qk, queries = [], [], [], []
    need(2)
    for n in range(chunks):
        rows = slice(n * CH, (n + 1) * CH)
        k = k_ref[rows, :].astype(F32)
        k = k * lax.rsqrt(jnp.sum(k * k, axis=-1, keepdims=True) + EPS)
        ks = split(k)
        keys.append(k)
        kk.append(mm3(ks, ks, NT))

    decay, grow, tail, end, strict_part, rate = {}, {}, {}, {}, {}, {}
    step, solved, prefixes = {}, {}, {}
    along_x = Gather4(xs, x, x_peers, xsend, xrecv)
    along_y = Gather4(ys, y, y_peers, ysend, yrecv, upward=True)
    need(5, 6)
    for h in range(2):
        mine = [(n, h) for n in range(chunks)]
        for n, h in mine:
            ld_row = ld_ref[h : h + 1, n * CH : (n + 1) * CH]
            ld_all = jnp.broadcast_to(ld_row, (CH, CH))
            wr_all = jnp.broadcast_to(wr_ref[h : h + 1, n * CH : (n + 1) * CH], (CH, CH))
            ld_col = jnp.sum(jnp.where(eye, ld_all, 0.0), axis=1, keepdims=True)
            cum_col = jnp.sum(jnp.where(causal, ld_all, 0.0), axis=1, keepdims=True)
            cum_row = jnp.sum(jnp.where(row <= col, ld_col, 0.0), axis=0, keepdims=True)
            rate[n, h] = jnp.sum(jnp.where(eye, wr_all, 0.0), axis=1, keepdims=True)
            total = jnp.sum(ld_row, axis=1, keepdims=True)
            decay[n, h] = jnp.where(causal, jnp.exp(jnp.where(causal, cum_col - cum_row, 0.0)), 0.0)
            grow[n, h] = jnp.exp(cum_col)
            tail[n, h] = jnp.exp(total - cum_col)
            end[n, h] = jnp.exp(total)
            strict_part[n, h] = jnp.where(strict, kk[n] * decay[n, h] * rate[n, h], 0.0)

        inverse = {}
        for p in mine:
            low = jnp.where((row // 2 == col // 2) & strict, strict_part[p], 0.0)
            inverse[p] = jnp.where(eye, 1.0, -low)
        width = 2
        while width < CH:
            mask = (row // (2 * width) == col // (2 * width)) & (row // width > col // width)
            inner = {}
            held = {}
            for p in mine:
                held[p] = split(inverse[p])
                inner[p] = mm3(split(jnp.where(mask, strict_part[p], 0.0)), held[p])
            for p in mine:
                inverse[p] = inverse[p] - mm3(held[p], split(inner[p]))
            width *= 2

        if h == 0:
            need(3)
        for n, h in mine:
            value = v_ref[n * CH : (n + 1) * CH, h * DV : (h + 1) * DV].astype(F32)
            sides = jnp.concatenate([keys[n] * (rate[n, h] * grow[n, h]), value * rate[n, h]], axis=1)
            solved[n, h] = split(mm3(inverse[n, h], sides))
        for n, h in mine:
            fed = mm3(split(keys[n] * tail[n, h]), solved[n, h], TN)
            step[n, h] = jnp.concatenate(
                [jnp.where(eye, end[n, h], 0.0) - fed[:, :DK], fed[:, DK:]], axis=1
            )
        first = compose(step[1, h], step[0, h])
        second = compose(step[3, h], step[2, h])
        whole = compose(second, first)
        xs[x, h] = whole.astype(BF16)
        if h == 0:
            meet()
        along_x.start(h)
        prefixes[1, h] = step[0, h]
        prefixes[2, h] = first
        prefixes[3, h] = (step[2, h], first)
    late()

    base, mapped = {}, {}
    need(1)
    for n in range(chunks):
        q = q_ref[n * CH : (n + 1) * CH, :].astype(F32)
        q = q * lax.rsqrt(jnp.sum(q * q, axis=-1, keepdims=True) + EPS) * DK ** (-0.5)
        queries.append(q)
        qk.append(mm3(split(q), split(keys[n]), NT))
    for n, h in pairs:
        scores = qk[n] * decay[n, h]
        seen = mm3(split(scores), solved[n, h])
        effective = queries[n] * grow[n, h] - seen[:, :DK]
        if n == 0:
            base[n, h], mapped[n, h] = seen[:, DK:], effective
        else:
            ahead = prefixes[n, h]
            if n == 3:
                ahead = compose(ahead[0], ahead[1])
            through = mm3(effective, ahead)
            base[n, h], mapped[n, h] = seen[:, DK:] + through[:, DK:], through[:, :DK]

    for h in range(2):
        along_x.finish(h)
        lower = compose(xs[1, h], xs[0, h])
        upper = compose(xs[3, h], xs[2, h])
        ys[y, h] = compose(upper, lower).astype(BF16)
        along_y.start(h)

    state = {}
    inside = {}
    start = jnp.where(
        lax.broadcasted_iota(jnp.int32, (DK, 2 * DK), 0)
        == lax.broadcasted_iota(jnp.int32, (DK, 2 * DK), 1),
        1.0,
        0.0,
    )
    for h in range(2):
        running = jnp.where(x > 0, xs[0, h].astype(F32), start)
        for other in range(1, 3):
            running = jnp.where(x > other, compose(xs[other, h], running), running)
        inside[h] = running
    gain = gain_ref[...]
    for h in range(2):
        along_y.finish(h)
        running = jnp.where(y > 0, ys[0, h, :, DK:].astype(F32), 0.0)
        for other in range(1, 3):
            after = mm2(ys[other, h, :, :DK], running) + ys[other, h, :, DK:].astype(F32)
            running = jnp.where(y > other, after, running)
        state[h] = split(mm3(inside[h][:, :DK], running) + inside[h][:, DK:])
        cols = slice(h * DV, (h + 1) * DV)
        for n in range(chunks):
            rows = slice(n * CH, (n + 1) * CH)
            readout = base[n, h] + mm3(mapped[n, h], state[h])
            scaled = readout * lax.rsqrt(jnp.mean(readout * readout, axis=-1, keepdims=True) + EPS)
            gate = g_ref[rows, cols].astype(F32)
            mixed = (scaled * gain * (gate / (1.0 + jnp.exp(-gate)))).astype(BF16)
            for i in range(4):
                at_chip = (2 * n + i // 2) * 32
                mix[i % 2, h, at_chip : at_chip + 32] = mixed[32 * i : 32 * i + 32]
        ready(h)

    def drain():
        along_x.drain()
        along_y.drain()

    return drain


class RingSum:
    def __init__(self, own, out, came, sem, ring):
        self.own, self.out, self.came, self.sem, self.ring = own, out, came, sem, ring
        self.sent = []

    def hop(self, way, step, part):
        return send_to(
            self.out.at[way, step, part],
            self.came.at[way, step, part],
            self.sem.at[0, way, step, part],
            self.sem.at[1, way, step, part],
            "exp",
            self.ring[way],
        )

    def launch(self, way, part):
        self.out[way, 0, part] = self.own[4, :, part * WIDE : (part + 1) * WIDE].astype(BF16)
        copy = self.hop(way, 0, part)
        copy.start()
        self.sent.append(copy)

    def run(self, prepare):
        for step in range(1, 4):
            prepare(step)
            for turn, way, part in turns()[2 * (PARTS // 2) :] + turns()[: 2 * (PARTS // 2)]:
                d = 4 - step if way == 0 else 4 + step
                total = self.own[d, :, part * WIDE : (part + 1) * WIDE]
                if step >= 2 or (step == 1 and turn == 0):
                    self.hop(way, step - 1, part).wait_recv()
                    total = total + self.came[way, step - 1, part].astype(F32)
                self.out[way, step, part] = total.astype(BF16)
                copy = self.hop(way, step, part)
                copy.start()
                self.sent.append(copy)
        prepare(4)

    def result(self, part):
        total = self.own[0, :, part * WIDE : (part + 1) * WIDE]
        for way in range(2):
            self.hop(way, 3, part).wait_recv()
            total = total + self.came[way, 3, part].astype(F32)
        return total

    def drain(self):
        for copy in self.sent:
            copy.wait_send()


def turns():
    some = PARTS // 2
    return [
        (turn, way, (way if turn == 0 else 1 - way) * some + i)
        for turn in range(2)
        for i in range(some)
        for way in range(2)
    ]


def kernel(*refs):
    inputs, o_ref, scratch = refs[:15], refs[15], refs[16:]
    held, scratch = scratch[:15], scratch[15:]
    (own, out, came, res, tokens, normed, table, mix, mix_in, xs, ys) = scratch[:11]
    (wsem, csem, msem, tsem, rsem, gsem, *seq_sems) = scratch[11:]
    (hid_ref, q, k, v, g, ld, wr, gain, ow, post_ref, ids_ref, route_ref, gw, uw, dw) = held
    weights = (8, 12, 13, 14)

    place = lax.axis_index("exp")
    z, core = lax.div(place, 2), lax.rem(place, 2)
    chips = [lax.rem(z + d, 8) * 2 + core for d in range(8)]
    sibling = z * 2 + (1 - core)
    ring = (chips[1], chips[7])
    turn_at = lax.axis_index("seq")
    x, y = lax.rem(turn_at, 4), lax.div(turn_at, 4)
    x_peers = [y * 4 + lax.rem(x + d, 4) for d in range(4)]
    y_peers = [lax.rem(y + d, 4) * 4 + x for d in range(4)]
    at = (x, y, x_peers, y_peers)
    ys[...] = jnp.zeros_like(ys)
    meet = greet(
        [("seq", peer) for peer in x_peers[1:] + y_peers[1:]]
        + [("exp", peer) for peer in chips[1:] + [sibling]]
    )

    loads, shared = [], []
    for i, (src, dst) in enumerate(zip(inputs, held)):
        if i in weights:
            flat = src if i == 8 else src.at[0]
            n = weights.index(i)
            shared.append(
                send_to(flat, dst.at[core], csem.at[0, n], csem.at[1, n], "exp", sibling)
            )
            dst, src = dst.at[core], flat
        loads.append(pltpu.make_async_copy(src, dst, wsem.at[i]))
    arriving = [
        send_to(
            held[i].at[1 - core], held[i].at[1 - core], csem.at[0, n], csem.at[1, n], "exp", sibling
        )
        for n, i in enumerate(weights)
    ]
    early, middle = (2, 5, 6, 3, 1), (10, 11, 4, 7, 0, 9)
    for i in early + middle:
        loads[i].start()

    def need(*which):
        for i in which:
            loads[i].wait()

    lane = lax.broadcasted_iota(jnp.int32, (32, 128), 1).astype(F32)
    sent = []

    def begin(copy):
        copy.start()
        sent.append(copy)

    def late():
        for i, copy in zip(weights, shared):
            loads[i].start()
            copy.start()
        for i in middle:
            loads[i].wait()
        ids = ids_ref[...].astype(F32)
        routes = route_ref[...].astype(F32)
        same = lax.broadcasted_iota(jnp.int32, (32, 32), 0) == lax.broadcasted_iota(
            jnp.int32, (32, 32), 1
        )
        shares = jnp.zeros((32, 128), F32)
        for j in range(4):
            named, share = (
                jnp.sum(jnp.where(same, a[j : j + 1, :], 0.0), axis=1, keepdims=True)
                for a in (ids, routes)
            )
            shares = shares + jnp.where(lane == named, share, 0.0)
        table[0] = shares.astype(BF16)
        for d in range(1, 8):
            begin(share_table(d))

    def share_table(d):
        return send_to(
            table.at[0], table.at[8 - d], tsem.at[0, 8 - d], tsem.at[1, 8 - d], "exp", chips[d]
        )

    def mix_copy(h):
        return send_to(
            mix.at[1 - core, h], mix_in.at[h], msem.at[0, h], msem.at[1, h], "exp", sibling
        )

    drain_seq = seq_part(
        q,
        k,
        v,
        g,
        ld,
        wr,
        gain,
        mix,
        xs,
        ys,
        seq_sems,
        at,
        need,
        meet,
        late,
        lambda h: begin(mix_copy(h)),
    )

    def mixed_rows(ref, offsets):
        rows = [pl.ds(pl.multiple_of(lax.rem(z + d, 8) * 32, 32), 32) for d in offsets]
        return jnp.concatenate(
            [jnp.concatenate([ref[h, r] for h in range(2)], axis=1) for r in rows], axis=0
        )

    def project(offsets):
        block = mm(mixed_rows(mix_in, offsets), ow[1 - core])
        for i, d in enumerate(offsets):
            own[0, d] = own[0, d] + block[32 * i : 32 * i + 32]

    loads[8].wait()
    block = mm(mixed_rows(mix.at[core], range(8)), ow[core])
    for d in range(8):
        own[0, d] = block[32 * d : 32 * d + 32]
    arriving[0].wait_recv()
    for h in range(2):
        mix_copy(h).wait_recv()
    first = RingSum(own.at[0], out.at[0], came.at[0], rsem.at[0], ring)
    project((4,))
    for turn, way, part in turns():
        if turn == 0:
            first.launch(way, part)
    first.run(lambda step: project(((4,), (3, 5), (2, 6), (1, 7), (0,))[step]))
    def onward(way, step, part):
        src = (8 - step) % 8 if way == 0 else step
        dst = 7 - step if way == 0 else step + 1
        return send_to(
            tokens.at[src, part],
            tokens.at[dst, part],
            gsem.at[0, way, step, part],
            gsem.at[1, way, step, part],
            "exp",
            ring[way],
        )

    def settle(offsets):
        for d in offsets:
            row = jnp.concatenate([tokens[d, part] for part in range(PARTS)], axis=1).astype(F32)
            scale = lax.rsqrt(jnp.mean(row * row, axis=-1, keepdims=True) + EPS)
            normed[d] = (row * scale * post_ref[...]).astype(BF16)

    def expert(offsets):
        for d in offsets:
            if d > 0:
                share_table(8 - d).wait_recv()
        shares = jnp.concatenate([table[d] for d in offsets], axis=0).astype(F32)
        lanes = lax.broadcasted_iota(jnp.int32, shares.shape, 1)
        hidden, share = [], []

        def close(e, gate, up):
            hidden.append((gate / (1.0 + jnp.exp(-gate)) * up).astype(BF16))
            share.append(
                jnp.sum(jnp.where(lanes == z * 2 + e, shares, 0.0), axis=1, keepdims=True)
            )

        def widen(e):
            picked = jnp.concatenate([normed[d] for d in offsets], axis=0)
            close(e, mm(picked, gw[e]), mm(picked, uw[e]))

        def widen_late():
            sums = [[0.0, 0.0], [0.0, 0.0]]
            square = 0.0
            for i in range(PARTS // 2):
                for way in range(2):
                    onward(way, 3, way * (PARTS // 2) + i).wait_recv()
                for part in (i, PARTS // 2 + i):
                    cols = slice(part * WIDE, (part + 1) * WIDE)
                    row = jnp.concatenate([tokens[d, part] for d in offsets], axis=0).astype(F32)
                    square = square + jnp.sum(row * row, axis=-1, keepdims=True)
                    row = (row * post_ref[:, cols]).astype(BF16)
                    for e in range(2):
                        for k, w in enumerate((gw, uw)):
                            sums[e][k] = sums[e][k] + mm(row, w[e, cols, :])
            scale = lax.rsqrt(square * (1.0 / D) + EPS)
            for e in range(2):
                close(e, sums[e][0] * scale, sums[e][1] * scale)

        def down(part):
            cols = slice(part * WIDE, (part + 1) * WIDE)
            total = sum(
                mm(hidden[e], dw[e, :, cols]).astype(BF16).astype(F32) * share[e]
                for e in range(2)
            )
            for i, d in enumerate(offsets):
                own[1, d, :, cols] = total[32 * i : 32 * i + 32]

        return widen, widen_late, down

    for part in (i + j for i in range(PARTS // 2) for j in (0, PARTS // 2)):
        cols = slice(part * WIDE, (part + 1) * WIDE)
        block = hid_ref[:, cols].astype(F32) + first.result(part)
        res[:, cols] = block
        tokens[0, part] = block.astype(BF16)
        ahead = 0 if part < PARTS // 2 else 1
        for way in (ahead, 1 - ahead):
            begin(onward(way, 0, part))
    settle((0,))
    for i in weights[1:]:
        loads[i].wait()
    for copy in arriving[1:]:
        copy.wait_recv()

    def pass_on(step):
        for turn, way, part in turns():
            onward(way, step - 1, part).wait_recv()
            if step < 3 or turn == 0:
                begin(onward(way, step, part))
        if step < 3:
            settle((8 - step, step))

    pass_on(1)
    near_widen, _, near_down = expert((0, 1, 7))
    near_widen(0)
    near_widen(1)
    pass_on(2)
    for part in range(PARTS):
        near_down(part)
    next_widen, _, next_down = expert((2, 6))
    next_widen(0)
    pass_on(3)
    next_widen(1)
    for part in range(PARTS):
        next_down(part)
    second = RingSum(own.at[1], out.at[1], came.at[1], rsem.at[1], ring)
    _, widen_late, down = expert((3, 4, 5))
    widen_late()
    for turn, way, part in turns():
        if turn == 0:
            down(part)
            second.launch(way, part)
    second.run(lambda step: None)
    for part in (i + j for i in range(PARTS // 2) for j in (0, PARTS // 2)):
        cols = slice(part * WIDE, (part + 1) * WIDE)
        o_ref[:, cols] = (res[:, cols] + second.result(part)).astype(BF16)
    for copy in sent + shared:
        copy.wait_send()
    first.drain()
    second.drain()
    drain_seq()


def per_device(*args):
    args = list(args)
    args[7] = args[7].reshape(1, DV)
    args[9] = args[9].reshape(1, D)
    args[10] = args[10].T
    args[11] = args[11].T
    slots = pltpu.VMEM((4, 2, DK, 2 * DK), BF16)
    both = {8: (2,) + args[8].shape}
    for i in (12, 13, 14):
        both[i] = (2,) + args[i].shape[1:]
    scratch = [pltpu.VMEM(both.get(i, a.shape), a.dtype) for i, a in enumerate(args)] + [
        pltpu.VMEM((2, 8, 32, D), F32),
        pltpu.VMEM((2, 2, 4, PARTS, 32, WIDE), BF16),
        pltpu.VMEM((2, 2, 4, PARTS, 32, WIDE), BF16),
        pltpu.VMEM((32, D), F32),
        pltpu.VMEM((8, PARTS, 32, WIDE), BF16),
        pltpu.VMEM((8, 32, D), BF16),
        pltpu.VMEM((8, 32, 128), BF16),
        pltpu.VMEM((2, 2, 256, DV), BF16),
        pltpu.VMEM((2, 256, DV), BF16),
        slots,
        slots,
        pltpu.SemaphoreType.DMA((15,)),
        pltpu.SemaphoreType.DMA((2, 4)),
        pltpu.SemaphoreType.DMA((2, 2)),
        pltpu.SemaphoreType.DMA((2, 8)),
        pltpu.SemaphoreType.DMA((2, 2, 2, 4, PARTS)),
        pltpu.SemaphoreType.DMA((2, 2, 4, PARTS)),
    ]
    return pl.pallas_call(
        kernel,
        out_shape=jax.ShapeDtypeStruct(args[0].shape, BF16),
        in_specs=[pl.BlockSpec(memory_space=pl.ANY)] * 15,
        out_specs=pl.BlockSpec(memory_space=pltpu.VMEM),
        scratch_shapes=scratch + [pltpu.SemaphoreType.DMA((4, 4))] * 4,
        compiler_params=pltpu.CompilerParams(
            collective_id=0, has_side_effects=True, vmem_limit_bytes=62 * 1024 * 1024
        ),
        name="layer",
    )(*args)


def solution(mesh):
    in_specs = (
        P(("seq", "exp"), None),
        P("seq", "exp"),
        P("seq", "exp"),
        P("seq", "exp"),
        P("seq", "exp"),
        P("exp", "seq"),
        P("exp", "seq"),
        P(),
        P("exp", None),
        P(),
        P(("seq", "exp"), None),
        P(("seq", "exp"), None),
        P("exp", None, None),
        P("exp", None, None),
        P("exp", None, None),
    )
    out_specs = P(("seq", "exp"), None)
    return jax.shard_map(
        per_device, mesh=mesh, in_specs=in_specs, out_specs=out_specs, check_vma=False
    )
```

```python
import functools

import jax
import jax.numpy as jnp
from jax import lax
from jax.experimental import pallas as pl
from jax.experimental.pallas import tpu as pltpu
from jax.sharding import PartitionSpec as P

D = 2048
FF = 512
DK = 128
DV = 128
EPS = 1e-06
CH = 128
PARTS = 4
WIDE = D // PARTS
F32 = jnp.float32
BF16 = jnp.bfloat16
MESH = pl.DeviceIdType.MESH
NN = (((1,), (0,)), ((), ()))
NT = (((1,), (1,)), ((), ()))
TN = (((0,), (0,)), ((), ()))


def mm(a, b, dims=NN):
    return lax.dot_general(a, b, dims, preferred_element_type=F32)


def split(a):
    hi = a.astype(BF16)
    return hi, (a - hi.astype(F32)).astype(BF16)


def mm3(a, b, dims=NN):
    ah, al = a if isinstance(a, tuple) else split(a)
    bh, bl = b if isinstance(b, tuple) else split(b)
    if dims != NN:
        return mm(ah, bh, dims) + (mm(ah, bl, dims) + mm(al, bh, dims))
    n = bh.shape[1]
    left = jnp.concatenate([ah, al], axis=1)
    if n > 128:
        return mm(left, jnp.concatenate([bh, bh], axis=0)) + mm(ah, bl)
    right = jnp.concatenate(
        [
            jnp.concatenate([bh, bl], axis=1),
            jnp.concatenate([bh, jnp.zeros_like(bl)], axis=1),
        ],
        axis=0,
    )
    both = mm(left, right)
    return both[:, :n] + both[:, n:]


def mm2(a, b, dims=NN):
    bh, bl = split(b)
    return mm(a, bh, dims) + mm(a, bl, dims)


def greet(peers):
    barrier = pltpu.get_barrier_semaphore()
    for axis, peer in peers:
        pl.semaphore_signal(barrier, inc=1, device_id={axis: peer}, device_id_type=MESH)
    return lambda: pl.semaphore_wait(barrier, len(peers))


def send_to(src, dst, send_sem, recv_sem, axis, peer):
    return pltpu.make_async_remote_copy(
        src_ref=src,
        dst_ref=dst,
        send_sem=send_sem,
        recv_sem=recv_sem,
        device_id={axis: peer},
        device_id_type=MESH,
    )


class Gather4:
    def __init__(self, slots, me, peers, ssem, rsem, upward=False):
        self.slots, self.me, self.peers, self.ssem, self.rsem = slots, me, peers, ssem, rsem
        self.upward = upward
        self.sent = []

    def copy(self, d, h, i):
        place = lax.rem(self.me + d, 4)
        piece = self.slots.at[place, h, pl.ds(i * 64, 64)]
        return piece, h * 2 + i

    def start(self, h):
        for i in range(2):
            piece, at = self.copy(0, h, i)
            for d in (2, 1, 3):
                copy = send_to(
                    piece, piece, self.ssem.at[d, at], self.rsem.at[d, at], "seq", self.peers[d]
                )
                self.when(self.me + d < 4, copy.start)
                self.sent.append((d, copy))

    def when(self, holds, act):
        if self.upward:
            pl.when(holds)(act)
        else:
            act()

    def finish(self, h):
        for d in (1, 3, 2):
            for i in range(2):
                piece, at = self.copy(4 - d, h, i)
                came = send_to(
                    piece, piece, self.ssem.at[d, at], self.rsem.at[d, at], "seq", self.peers[d]
                )
                self.when(self.me >= d, came.wait_recv)

    def drain(self):
        for d, copy in self.sent:
            self.when(self.me + d < 4, copy.wait_send)


def compose(later, earlier):
    later = later.astype(F32)
    earlier = earlier.astype(F32)
    joined = mm3(later[:, :DK], earlier)
    return joined + jnp.concatenate([jnp.zeros((DK, DK), F32), later[:, DK:]], axis=1)


def seq_part(q_ref, k_ref, v_ref, g_ref, ld_ref, wr_ref, gain_ref, mix, xs, ys, sems, at, need, meet, late, ready):
    xsend, xrecv, ysend, yrecv = sems
    x, y, x_peers, y_peers = at
    chunks = q_ref.shape[0] // CH
    row = lax.broadcasted_iota(jnp.int32, (CH, CH), 0)
    col = lax.broadcasted_iota(jnp.int32, (CH, CH), 1)
    eye = row == col
    causal = row >= col
    strict = row > col
    pairs = [(n, h) for n in range(chunks) for h in range(2)]

    keys, kk, qk, queries = [], [], [], []
    need(2)
    for n in range(chunks):
        rows = slice(n * CH, (n + 1) * CH)
        k = k_ref[rows, :].astype(F32)
        k = k * lax.rsqrt(jnp.sum(k * k, axis=-1, keepdims=True) + EPS)
        ks = split(k)
        keys.append(k)
        kk.append(mm3(ks, ks, NT))

    decay, grow, tail, end, strict_part, rate = {}, {}, {}, {}, {}, {}
    step, solved, prefixes = {}, {}, {}
    along_x = Gather4(xs, x, x_peers, xsend, xrecv)
    along_y = Gather4(ys, y, y_peers, ysend, yrecv, upward=True)
    need(5, 6)
    for h in range(2):
        mine = [(n, h) for n in range(chunks)]
        for n, h in mine:
            ld_row = ld_ref[h : h + 1, n * CH : (n + 1) * CH]
            ld_all = jnp.broadcast_to(ld_row, (CH, CH))
            wr_all = jnp.broadcast_to(wr_ref[h : h + 1, n * CH : (n + 1) * CH], (CH, CH))
            ld_col = jnp.sum(jnp.where(eye, ld_all, 0.0), axis=1, keepdims=True)
            cum_col = jnp.sum(jnp.where(causal, ld_all, 0.0), axis=1, keepdims=True)
            cum_row = jnp.sum(jnp.where(row <= col, ld_col, 0.0), axis=0, keepdims=True)
            rate[n, h] = jnp.sum(jnp.where(eye, wr_all, 0.0), axis=1, keepdims=True)
            total = jnp.sum(ld_row, axis=1, keepdims=True)
            decay[n, h] = jnp.where(causal, jnp.exp(jnp.where(causal, cum_col - cum_row, 0.0)), 0.0)
            grow[n, h] = jnp.exp(cum_col)
            tail[n, h] = jnp.exp(total - cum_col)
            end[n, h] = jnp.exp(total)
            strict_part[n, h] = jnp.where(strict, kk[n] * decay[n, h] * rate[n, h], 0.0)

        inverse = {}
        for p in mine:
            low = jnp.where((row // 2 == col // 2) & strict, strict_part[p], 0.0)
            inverse[p] = jnp.where(eye, 1.0, -low)
        width = 2
        while width < CH:
            mask = (row // (4 * width) == col // (4 * width)) & (row // width > col // width)
            held, lower, rest, twice = {}, {}, {}, {}
            for p in mine:
                held[p] = split(inverse[p])
                lower[p] = split(mm3(held[p], split(jnp.where(mask, strict_part[p], 0.0))))
            for p in mine:
                rest[p] = inverse[p] - mm3(lower[p], held[p])
                twice[p] = split(mm3(lower[p], lower[p]))
            for p in mine:
                inverse[p] = rest[p] + mm3(twice[p], split(rest[p]))
            width *= 4

        if h == 0:
            need(3)
        for n, h in mine:
            value = v_ref[n * CH : (n + 1) * CH, h * DV : (h + 1) * DV].astype(F32)
            sides = jnp.concatenate([keys[n] * (rate[n, h] * grow[n, h]), value * rate[n, h]], axis=1)
            solved[n, h] = split(mm3(inverse[n, h], sides))
        for n, h in mine:
            fed = mm3(split(keys[n] * tail[n, h]), solved[n, h], TN)
            step[n, h] = jnp.concatenate(
                [jnp.where(eye, end[n, h], 0.0) - fed[:, :DK], fed[:, DK:]], axis=1
            )
        first = compose(step[1, h], step[0, h])
        second = compose(step[3, h], step[2, h])
        whole = compose(second, first)
        xs[x, h] = whole.astype(BF16)
        if h == 0:
            meet()
        along_x.start(h)
        prefixes[1, h] = step[0, h]
        prefixes[2, h] = first
        prefixes[3, h] = (step[2, h], first)
    late()

    base, mapped = {}, {}
    need(1)
    for n in range(chunks):
        q = q_ref[n * CH : (n + 1) * CH, :].astype(F32)
        q = q * lax.rsqrt(jnp.sum(q * q, axis=-1, keepdims=True) + EPS) * DK ** (-0.5)
        queries.append(q)
        qk.append(mm3(split(q), split(keys[n]), NT))
    for n, h in pairs:
        scores = qk[n] * decay[n, h]
        seen = mm3(split(scores), solved[n, h])
        effective = queries[n] * grow[n, h] - seen[:, :DK]
        if n == 0:
            base[n, h], mapped[n, h] = seen[:, DK:], effective
        else:
            ahead = prefixes[n, h]
            if n == 3:
                ahead = compose(ahead[0], ahead[1])
            through = mm3(effective, ahead)
            base[n, h], mapped[n, h] = seen[:, DK:] + through[:, DK:], through[:, :DK]

    for h in range(2):
        along_x.finish(h)
        lower = compose(xs[1, h], xs[0, h])
        upper = compose(xs[3, h], xs[2, h])
        ys[y, h] = compose(upper, lower).astype(BF16)
        along_y.start(h)

    state = {}
    inside = {}
    start = jnp.where(
        lax.broadcasted_iota(jnp.int32, (DK, 2 * DK), 0)
        == lax.broadcasted_iota(jnp.int32, (DK, 2 * DK), 1),
        1.0,
        0.0,
    )
    for h in range(2):
        running = jnp.where(x > 0, xs[0, h].astype(F32), start)
        for other in range(1, 3):
            running = jnp.where(x > other, compose(xs[other, h], running), running)
        inside[h] = running
    gain = gain_ref[...]
    for h in range(2):
        along_y.finish(h)
        running = jnp.where(y > 0, ys[0, h, :, DK:].astype(F32), 0.0)
        for other in range(1, 3):
            after = mm2(ys[other, h, :, :DK], running) + ys[other, h, :, DK:].astype(F32)
            running = jnp.where(y > other, after, running)
        state[h] = split(mm3(inside[h][:, :DK], running) + inside[h][:, DK:])
        cols = slice(h * DV, (h + 1) * DV)
        for n in range(chunks):
            rows = slice(n * CH, (n + 1) * CH)
            readout = base[n, h] + mm3(mapped[n, h], state[h])
            scaled = readout * lax.rsqrt(jnp.mean(readout * readout, axis=-1, keepdims=True) + EPS)
            gate = g_ref[rows, cols].astype(F32)
            mixed = (scaled * gain * (gate / (1.0 + jnp.exp(-gate)))).astype(BF16)
            for i in range(4):
                at_chip = (2 * n + i // 2) * 32
                mix[i % 2, h, at_chip : at_chip + 32] = mixed[32 * i : 32 * i + 32]
        ready(h)

    def drain():
        along_x.drain()
        along_y.drain()

    return drain


class RingSum:
    def __init__(self, own, out, came, sem, ring):
        self.own, self.out, self.came, self.sem, self.ring = own, out, came, sem, ring
        self.sent = []

    def hop(self, way, step, part):
        return send_to(
            self.out.at[way, step, part],
            self.came.at[way, step, part],
            self.sem.at[0, way, step, part],
            self.sem.at[1, way, step, part],
            "exp",
            self.ring[way],
        )

    def launch(self, way, part):
        self.out[way, 0, part] = self.own[4, :, part * WIDE : (part + 1) * WIDE].astype(BF16)
        copy = self.hop(way, 0, part)
        copy.start()
        self.sent.append(copy)

    def run(self, prepare):
        for step in range(1, 4):
            prepare(step)
            for turn, way, part in turns()[2 * (PARTS // 2) :] + turns()[: 2 * (PARTS // 2)]:
                d = 4 - step if way == 0 else 4 + step
                total = self.own[d, :, part * WIDE : (part + 1) * WIDE]
                if step >= 2 or (step == 1 and turn == 0):
                    self.hop(way, step - 1, part).wait_recv()
                    total = total + self.came[way, step - 1, part].astype(F32)
                self.out[way, step, part] = total.astype(BF16)
                copy = self.hop(way, step, part)
                copy.start()
                self.sent.append(copy)
        prepare(4)

    def result(self, part):
        total = self.own[0, :, part * WIDE : (part + 1) * WIDE]
        for way in range(2):
            self.hop(way, 3, part).wait_recv()
            total = total + self.came[way, 3, part].astype(F32)
        return total

    def drain(self):
        for copy in self.sent:
            copy.wait_send()


def turns():
    some = PARTS // 2
    return [
        (turn, way, (way if turn == 0 else 1 - way) * some + i)
        for turn in range(2)
        for i in range(some)
        for way in range(2)
    ]


def kernel(*refs):
    inputs, o_ref, scratch = refs[:15], refs[15], refs[16:]
    held, scratch = scratch[:15], scratch[15:]
    (own, out, came, res, tokens, normed, table, mix, mix_in, xs, ys) = scratch[:11]
    (wsem, csem, msem, tsem, rsem, gsem, *seq_sems) = scratch[11:]
    (hid_ref, q, k, v, g, ld, wr, gain, ow, post_ref, ids_ref, route_ref, gw, uw, dw) = held
    weights = (8, 12, 13, 14)

    place = lax.axis_index("exp")
    z, core = lax.div(place, 2), lax.rem(place, 2)
    chips = [lax.rem(z + d, 8) * 2 + core for d in range(8)]
    sibling = z * 2 + (1 - core)
    ring = (chips[1], chips[7])
    turn_at = lax.axis_index("seq")
    x, y = lax.rem(turn_at, 4), lax.div(turn_at, 4)
    x_peers = [y * 4 + lax.rem(x + d, 4) for d in range(4)]
    y_peers = [lax.rem(y + d, 4) * 4 + x for d in range(4)]
    at = (x, y, x_peers, y_peers)
    ys[...] = jnp.zeros_like(ys)
    meet = greet(
        [("seq", peer) for peer in x_peers[1:] + y_peers[1:]]
        + [("exp", peer) for peer in chips[1:] + [sibling]]
    )

    loads, shared = [], []
    for i, (src, dst) in enumerate(zip(inputs, held)):
        if i in weights:
            flat = src if i == 8 else src.at[0]
            n = weights.index(i)
            shared.append(
                send_to(flat, dst.at[core], csem.at[0, n], csem.at[1, n], "exp", sibling)
            )
            dst, src = dst.at[core], flat
        loads.append(pltpu.make_async_copy(src, dst, wsem.at[i]))
    arriving = [
        send_to(
            held[i].at[1 - core], held[i].at[1 - core], csem.at[0, n], csem.at[1, n], "exp", sibling
        )
        for n, i in enumerate(weights)
    ]
    early, middle = (2, 5, 6, 3, 1), (10, 11, 4, 7, 0, 9)
    for i in early + middle:
        loads[i].start()

    def need(*which):
        for i in which:
            loads[i].wait()

    lane = lax.broadcasted_iota(jnp.int32, (32, 128), 1).astype(F32)
    sent = []

    def begin(copy):
        copy.start()
        sent.append(copy)

    def late():
        for i, copy in zip(weights, shared):
            loads[i].start()
            copy.start()
        for i in middle:
            loads[i].wait()
        ids = ids_ref[...].astype(F32)
        routes = route_ref[...].astype(F32)
        same = lax.broadcasted_iota(jnp.int32, (32, 32), 0) == lax.broadcasted_iota(
            jnp.int32, (32, 32), 1
        )
        shares = jnp.zeros((32, 128), F32)
        for j in range(4):
            named, share = (
                jnp.sum(jnp.where(same, a[j : j + 1, :], 0.0), axis=1, keepdims=True)
                for a in (ids, routes)
            )
            shares = shares + jnp.where(lane == named, share, 0.0)
        table[0] = shares.astype(BF16)
        for d in range(1, 8):
            begin(share_table(d))

    def share_table(d):
        return send_to(
            table.at[0], table.at[8 - d], tsem.at[0, 8 - d], tsem.at[1, 8 - d], "exp", chips[d]
        )

    def mix_copy(h):
        return send_to(
            mix.at[1 - core, h], mix_in.at[h], msem.at[0, h], msem.at[1, h], "exp", sibling
        )

    drain_seq = seq_part(
        q,
        k,
        v,
        g,
        ld,
        wr,
        gain,
        mix,
        xs,
        ys,
        seq_sems,
        at,
        need,
        meet,
        late,
        lambda h: begin(mix_copy(h)),
    )

    def mixed_rows(ref, offsets):
        rows = [pl.ds(pl.multiple_of(lax.rem(z + d, 8) * 32, 32), 32) for d in offsets]
        return jnp.concatenate(
            [jnp.concatenate([ref[h, r] for h in range(2)], axis=1) for r in rows], axis=0
        )

    def project(offsets):
        block = mm(mixed_rows(mix_in, offsets), ow[1 - core])
        for i, d in enumerate(offsets):
            own[0, d] = own[0, d] + block[32 * i : 32 * i + 32]

    loads[8].wait()
    block = mm(mixed_rows(mix.at[core], range(8)), ow[core])
    for d in range(8):
        own[0, d] = block[32 * d : 32 * d + 32]
    arriving[0].wait_recv()
    for h in range(2):
        mix_copy(h).wait_recv()
    first = RingSum(own.at[0], out.at[0], came.at[0], rsem.at[0], ring)
    project((4,))
    for turn, way, part in turns():
        if turn == 0:
            first.launch(way, part)
    first.run(lambda step: project(((4,), (3, 5), (2, 6), (1, 7), (0,))[step]))
    def onward(way, step, part):
        src = (8 - step) % 8 if way == 0 else step
        dst = 7 - step if way == 0 else step + 1
        return send_to(
            tokens.at[src, part],
            tokens.at[dst, part],
            gsem.at[0, way, step, part],
            gsem.at[1, way, step, part],
            "exp",
            ring[way],
        )

    def settle(offsets):
        for d in offsets:
            row = jnp.concatenate([tokens[d, part] for part in range(PARTS)], axis=1).astype(F32)
            scale = lax.rsqrt(jnp.mean(row * row, axis=-1, keepdims=True) + EPS)
            normed[d] = (row * scale * post_ref[...]).astype(BF16)

    def expert(offsets):
        for d in offsets:
            if d > 0:
                share_table(8 - d).wait_recv()
        shares = jnp.concatenate([table[d] for d in offsets], axis=0).astype(F32)
        lanes = lax.broadcasted_iota(jnp.int32, shares.shape, 1)
        hidden, share = [], []

        def close(e, gate, up):
            hidden.append((gate / (1.0 + jnp.exp(-gate)) * up).astype(BF16))
            share.append(
                jnp.sum(jnp.where(lanes == z * 2 + e, shares, 0.0), axis=1, keepdims=True)
            )

        def widen(e):
            picked = jnp.concatenate([normed[d] for d in offsets], axis=0)
            close(e, mm(picked, gw[e]), mm(picked, uw[e]))

        def widen_late():
            sums = [[0.0, 0.0], [0.0, 0.0]]
            square = 0.0
            for i in range(PARTS // 2):
                for way in range(2):
                    onward(way, 3, way * (PARTS // 2) + i).wait_recv()
                for part in (i, PARTS // 2 + i):
                    cols = slice(part * WIDE, (part + 1) * WIDE)
                    row = jnp.concatenate([tokens[d, part] for d in offsets], axis=0).astype(F32)
                    square = square + jnp.sum(row * row, axis=-1, keepdims=True)
                    row = (row * post_ref[:, cols]).astype(BF16)
                    for e in range(2):
                        for k, w in enumerate((gw, uw)):
                            sums[e][k] = sums[e][k] + mm(row, w[e, cols, :])
            scale = lax.rsqrt(square * (1.0 / D) + EPS)
            for e in range(2):
                close(e, sums[e][0] * scale, sums[e][1] * scale)

        def down(part):
            cols = slice(part * WIDE, (part + 1) * WIDE)
            total = sum(
                mm(hidden[e], dw[e, :, cols]).astype(BF16).astype(F32) * share[e]
                for e in range(2)
            )
            for i, d in enumerate(offsets):
                own[1, d, :, cols] = total[32 * i : 32 * i + 32]

        return widen, widen_late, down

    for part in (i + j for i in range(PARTS // 2) for j in (0, PARTS // 2)):
        cols = slice(part * WIDE, (part + 1) * WIDE)
        block = hid_ref[:, cols].astype(F32) + first.result(part)
        res[:, cols] = block
        tokens[0, part] = block.astype(BF16)
        ahead = 0 if part < PARTS // 2 else 1
        for way in (ahead, 1 - ahead):
            begin(onward(way, 0, part))
    settle((0,))
    for i in weights[1:]:
        loads[i].wait()
    for copy in arriving[1:]:
        copy.wait_recv()

    def pass_on(step):
        for turn, way, part in turns():
            onward(way, step - 1, part).wait_recv()
            if step < 3 or turn == 0:
                begin(onward(way, step, part))
        if step < 3:
            settle((8 - step, step))

    pass_on(1)
    near_widen, _, near_down = expert((0, 1, 7))
    near_widen(0)
    near_widen(1)
    pass_on(2)
    for part in range(PARTS):
        near_down(part)
    next_widen, _, next_down = expert((2, 6))
    next_widen(0)
    pass_on(3)
    next_widen(1)
    for part in range(PARTS):
        next_down(part)
    second = RingSum(own.at[1], out.at[1], came.at[1], rsem.at[1], ring)
    _, widen_late, down = expert((3, 4, 5))
    widen_late()
    for turn, way, part in turns():
        if turn == 0:
            down(part)
            second.launch(way, part)
    second.run(lambda step: None)
    for part in (i + j for i in range(PARTS // 2) for j in (0, PARTS // 2)):
        cols = slice(part * WIDE, (part + 1) * WIDE)
        o_ref[:, cols] = (res[:, cols] + second.result(part)).astype(BF16)
    for copy in sent + shared:
        copy.wait_send()
    first.drain()
    second.drain()
    drain_seq()


def per_device(*args):
    args = list(args)
    args[7] = args[7].reshape(1, DV)
    args[9] = args[9].reshape(1, D)
    args[10] = args[10].T
    args[11] = args[11].T
    slots = pltpu.VMEM((4, 2, DK, 2 * DK), BF16)
    both = {8: (2,) + args[8].shape}
    for i in (12, 13, 14):
        both[i] = (2,) + args[i].shape[1:]
    scratch = [pltpu.VMEM(both.get(i, a.shape), a.dtype) for i, a in enumerate(args)] + [
        pltpu.VMEM((2, 8, 32, D), F32),
        pltpu.VMEM((2, 2, 4, PARTS, 32, WIDE), BF16),
        pltpu.VMEM((2, 2, 4, PARTS, 32, WIDE), BF16),
        pltpu.VMEM((32, D), F32),
        pltpu.VMEM((8, PARTS, 32, WIDE), BF16),
        pltpu.VMEM((8, 32, D), BF16),
        pltpu.VMEM((8, 32, 128), BF16),
        pltpu.VMEM((2, 2, 256, DV), BF16),
        pltpu.VMEM((2, 256, DV), BF16),
        slots,
        slots,
        pltpu.SemaphoreType.DMA((15,)),
        pltpu.SemaphoreType.DMA((2, 4)),
        pltpu.SemaphoreType.DMA((2, 2)),
        pltpu.SemaphoreType.DMA((2, 8)),
        pltpu.SemaphoreType.DMA((2, 2, 2, 4, PARTS)),
        pltpu.SemaphoreType.DMA((2, 2, 4, PARTS)),
    ]
    return pl.pallas_call(
        kernel,
        out_shape=jax.ShapeDtypeStruct(args[0].shape, BF16),
        in_specs=[pl.BlockSpec(memory_space=pl.ANY)] * 15,
        out_specs=pl.BlockSpec(memory_space=pltpu.VMEM),
        scratch_shapes=scratch + [pltpu.SemaphoreType.DMA((4, 4))] * 4,
        compiler_params=pltpu.CompilerParams(
            collective_id=0, has_side_effects=True, vmem_limit_bytes=62 * 1024 * 1024
        ),
        name="layer",
    )(*args)


def solution(mesh):
    in_specs = (
        P(("seq", "exp"), None),
        P("seq", "exp"),
        P("seq", "exp"),
        P("seq", "exp"),
        P("seq", "exp"),
        P("exp", "seq"),
        P("exp", "seq"),
        P(),
        P("exp", None),
        P(),
        P(("seq", "exp"), None),
        P(("seq", "exp"), None),
        P("exp", None, None),
        P("exp", None, None),
        P("exp", None, None),
    )
    out_specs = P(("seq", "exp"), None)
    return jax.shard_map(
        per_device, mesh=mesh, in_specs=in_specs, out_specs=out_specs, check_vma=False
    )
```

```python
import functools

import jax
import jax.numpy as jnp
from jax import lax
from jax.experimental import pallas as pl
from jax.experimental.pallas import tpu as pltpu
from jax.sharding import PartitionSpec as P

D = 2048
FF = 512
DK = 128
DV = 128
EPS = 1e-06
CH = 128
PARTS = 4
WIDE = D // PARTS
F32 = jnp.float32
BF16 = jnp.bfloat16
MESH = pl.DeviceIdType.MESH
NN = (((1,), (0,)), ((), ()))
NT = (((1,), (1,)), ((), ()))
TN = (((0,), (0,)), ((), ()))


def mm(a, b, dims=NN):
    return lax.dot_general(a, b, dims, preferred_element_type=F32)


def split(a):
    hi = a.astype(BF16)
    return hi, (a - hi.astype(F32)).astype(BF16)


def mm3(a, b, dims=NN):
    ah, al = a if isinstance(a, tuple) else split(a)
    bh, bl = b if isinstance(b, tuple) else split(b)
    if dims != NN:
        return mm(ah, bh, dims) + (mm(ah, bl, dims) + mm(al, bh, dims))
    n = bh.shape[1]
    left = jnp.concatenate([ah, al], axis=1)
    if n > 128:
        return mm(left, jnp.concatenate([bh, bh], axis=0)) + mm(ah, bl)
    right = jnp.concatenate(
        [
            jnp.concatenate([bh, bl], axis=1),
            jnp.concatenate([bh, jnp.zeros_like(bl)], axis=1),
        ],
        axis=0,
    )
    both = mm(left, right)
    return both[:, :n] + both[:, n:]


def mm2(a, b, dims=NN):
    bh, bl = split(b)
    return mm(a, bh, dims) + mm(a, bl, dims)


def greet(peers):
    barrier = pltpu.get_barrier_semaphore()
    for axis, peer in peers:
        pl.semaphore_signal(barrier, inc=1, device_id={axis: peer}, device_id_type=MESH)
    return lambda: pl.semaphore_wait(barrier, len(peers))


def send_to(src, dst, send_sem, recv_sem, axis, peer):
    return pltpu.make_async_remote_copy(
        src_ref=src,
        dst_ref=dst,
        send_sem=send_sem,
        recv_sem=recv_sem,
        device_id={axis: peer},
        device_id_type=MESH,
    )


class Gather4:
    def __init__(self, slots, me, peers, ssem, rsem, upward=False):
        self.slots, self.me, self.peers, self.ssem, self.rsem = slots, me, peers, ssem, rsem
        self.upward = upward
        self.sent = []

    def copy(self, d, h, i):
        place = lax.rem(self.me + d, 4)
        piece = self.slots.at[place, h, pl.ds(i * 64, 64)]
        return piece, h * 2 + i

    def start(self, h):
        for i in range(2):
            piece, at = self.copy(0, h, i)
            for d in (2, 1, 3):
                copy = send_to(
                    piece, piece, self.ssem.at[d, at], self.rsem.at[d, at], "seq", self.peers[d]
                )
                self.when(self.me + d < 4, copy.start)
                self.sent.append((d, copy))

    def when(self, holds, act):
        if self.upward:
            pl.when(holds)(act)
        else:
            act()

    def finish(self, h):
        for d in (1, 3, 2):
            for i in range(2):
                piece, at = self.copy(4 - d, h, i)
                came = send_to(
                    piece, piece, self.ssem.at[d, at], self.rsem.at[d, at], "seq", self.peers[d]
                )
                self.when(self.me >= d, came.wait_recv)

    def drain(self):
        for d, copy in self.sent:
            self.when(self.me + d < 4, copy.wait_send)


def compose(later, earlier):
    later = later.astype(F32)
    earlier = earlier.astype(F32)
    joined = mm3(later[:, :DK], earlier)
    return joined + jnp.concatenate([jnp.zeros((DK, DK), F32), later[:, DK:]], axis=1)


def seq_part(q_ref, k_ref, v_ref, g_ref, ld_ref, wr_ref, gain_ref, mix, xs, ys, sems, at, need, meet, give, late, ready):
    xsend, xrecv, ysend, yrecv = sems
    x, y, x_peers, y_peers = at
    chunks = q_ref.shape[0] // CH
    row = lax.broadcasted_iota(jnp.int32, (CH, CH), 0)
    col = lax.broadcasted_iota(jnp.int32, (CH, CH), 1)
    eye = row == col
    causal = row >= col
    strict = row > col
    pairs = [(n, h) for n in range(chunks) for h in range(2)]

    keys, kk, qk, queries = [], [], [], []
    need(2)
    for n in range(chunks):
        rows = slice(n * CH, (n + 1) * CH)
        k = k_ref[rows, :].astype(F32)
        k = k * lax.rsqrt(jnp.sum(k * k, axis=-1, keepdims=True) + EPS)
        ks = split(k)
        keys.append(k)
        kk.append(mm3(ks, ks, NT))

    decay, grow, tail, end, strict_part, rate = {}, {}, {}, {}, {}, {}
    step, solved, prefixes = {}, {}, {}
    along_x = Gather4(xs, x, x_peers, xsend, xrecv)
    along_y = Gather4(ys, y, y_peers, ysend, yrecv, upward=True)
    need(5, 6)
    for h in range(2):
        mine = [(n, h) for n in range(chunks)]
        for n, h in mine:
            ld_row = ld_ref[h : h + 1, n * CH : (n + 1) * CH]
            ld_all = jnp.broadcast_to(ld_row, (CH, CH))
            wr_all = jnp.broadcast_to(wr_ref[h : h + 1, n * CH : (n + 1) * CH], (CH, CH))
            ld_col = jnp.sum(jnp.where(eye, ld_all, 0.0), axis=1, keepdims=True)
            cum_col = jnp.sum(jnp.where(causal, ld_all, 0.0), axis=1, keepdims=True)
            cum_row = jnp.sum(jnp.where(row <= col, ld_col, 0.0), axis=0, keepdims=True)
            rate[n, h] = jnp.sum(jnp.where(eye, wr_all, 0.0), axis=1, keepdims=True)
            total = jnp.sum(ld_row, axis=1, keepdims=True)
            decay[n, h] = jnp.where(causal, jnp.exp(jnp.where(causal, cum_col - cum_row, 0.0)), 0.0)
            grow[n, h] = jnp.exp(cum_col)
            tail[n, h] = jnp.exp(total - cum_col)
            end[n, h] = jnp.exp(total)
            strict_part[n, h] = jnp.where(strict, kk[n] * decay[n, h] * rate[n, h], 0.0)

        inverse = {}
        for p in mine:
            low = jnp.where((row // 2 == col // 2) & strict, strict_part[p], 0.0)
            inverse[p] = jnp.where(eye, 1.0, -low)
        width = 2
        while width < CH:
            mask = (row // (4 * width) == col // (4 * width)) & (row // width > col // width)
            held, lower, rest, twice = {}, {}, {}, {}
            for p in mine:
                held[p] = split(inverse[p])
                lower[p] = split(mm3(held[p], split(jnp.where(mask, strict_part[p], 0.0))))
            for p in mine:
                rest[p] = inverse[p] - mm3(lower[p], held[p])
                twice[p] = split(mm3(lower[p], lower[p]))
            for p in mine:
                inverse[p] = rest[p] + mm3(twice[p], split(rest[p]))
            width *= 4

        if h == 0:
            need(3)
        for n, h in mine:
            value = v_ref[n * CH : (n + 1) * CH, h * DV : (h + 1) * DV].astype(F32)
            sides = jnp.concatenate([keys[n] * (rate[n, h] * grow[n, h]), value * rate[n, h]], axis=1)
            solved[n, h] = split(mm3(inverse[n, h], sides))
        for n, h in mine:
            fed = mm3(split(keys[n] * tail[n, h]), solved[n, h], TN)
            step[n, h] = jnp.concatenate(
                [jnp.where(eye, end[n, h], 0.0) - fed[:, :DK], fed[:, DK:]], axis=1
            )
        first = compose(step[1, h], step[0, h])
        second = compose(step[3, h], step[2, h])
        whole = compose(second, first)
        xs[x, h] = whole.astype(BF16)
        if h == 0:
            meet()
        along_x.start(h)
        if h == 0:
            give()
        prefixes[1, h] = step[0, h]
        prefixes[2, h] = first
        prefixes[3, h] = (step[2, h], first)
    late()

    base, mapped = {}, {}
    need(1)
    for n in range(chunks):
        q = q_ref[n * CH : (n + 1) * CH, :].astype(F32)
        q = q * lax.rsqrt(jnp.sum(q * q, axis=-1, keepdims=True) + EPS) * DK ** (-0.5)
        queries.append(q)
        qk.append(mm3(split(q), split(keys[n]), NT))
    for n, h in pairs:
        scores = qk[n] * decay[n, h]
        seen = mm3(split(scores), solved[n, h])
        effective = queries[n] * grow[n, h] - seen[:, :DK]
        if n == 0:
            base[n, h], mapped[n, h] = seen[:, DK:], effective
        else:
            ahead = prefixes[n, h]
            if n == 3:
                ahead = compose(ahead[0], ahead[1])
            through = mm3(effective, ahead)
            base[n, h], mapped[n, h] = seen[:, DK:] + through[:, DK:], through[:, :DK]

    for h in range(2):
        along_x.finish(h)
        lower = compose(xs[1, h], xs[0, h])
        upper = compose(xs[3, h], xs[2, h])
        ys[y, h] = compose(upper, lower).astype(BF16)
        along_y.start(h)

    state = {}
    inside = {}
    start = jnp.where(
        lax.broadcasted_iota(jnp.int32, (DK, 2 * DK), 0)
        == lax.broadcasted_iota(jnp.int32, (DK, 2 * DK), 1),
        1.0,
        0.0,
    )
    for h in range(2):
        running = jnp.where(x > 0, xs[0, h].astype(F32), start)
        for other in range(1, 3):
            running = jnp.where(x > other, compose(xs[other, h], running), running)
        inside[h] = running
    gain = gain_ref[...]
    for h in range(2):
        along_y.finish(h)
        running = jnp.where(y > 0, ys[0, h, :, DK:].astype(F32), 0.0)
        for other in range(1, 3):
            after = mm2(ys[other, h, :, :DK], running) + ys[other, h, :, DK:].astype(F32)
            running = jnp.where(y > other, after, running)
        state[h] = split(mm3(inside[h][:, :DK], running) + inside[h][:, DK:])
        cols = slice(h * DV, (h + 1) * DV)
        for n in range(chunks):
            rows = slice(n * CH, (n + 1) * CH)
            readout = base[n, h] + mm3(mapped[n, h], state[h])
            scaled = readout * lax.rsqrt(jnp.mean(readout * readout, axis=-1, keepdims=True) + EPS)
            gate = g_ref[rows, cols].astype(F32)
            mixed = (scaled * gain * (gate / (1.0 + jnp.exp(-gate)))).astype(BF16)
            for i in range(4):
                at_chip = (2 * n + i // 2) * 32
                mix[i % 2, h, at_chip : at_chip + 32] = mixed[32 * i : 32 * i + 32]
        ready(h)

    def drain():
        along_x.drain()
        along_y.drain()

    return drain


class RingSum:
    def __init__(self, own, out, came, sem, ring):
        self.own, self.out, self.came, self.sem, self.ring = own, out, came, sem, ring
        self.sent = []

    def hop(self, way, step, part):
        return send_to(
            self.out.at[way, step, part],
            self.came.at[way, step, part],
            self.sem.at[0, way, step, part],
            self.sem.at[1, way, step, part],
            "exp",
            self.ring[way],
        )

    def launch(self, way, part):
        self.out[way, 0, part] = self.own[4, :, part * WIDE : (part + 1) * WIDE].astype(BF16)
        copy = self.hop(way, 0, part)
        copy.start()
        self.sent.append(copy)

    def run(self, prepare):
        for step in range(1, 4):
            prepare(step)
            for turn, way, part in turns()[2 * (PARTS // 2) :] + turns()[: 2 * (PARTS // 2)]:
                d = 4 - step if way == 0 else 4 + step
                total = self.own[d, :, part * WIDE : (part + 1) * WIDE]
                if step >= 2 or (step == 1 and turn == 0):
                    self.hop(way, step - 1, part).wait_recv()
                    total = total + self.came[way, step - 1, part].astype(F32)
                self.out[way, step, part] = total.astype(BF16)
                copy = self.hop(way, step, part)
                copy.start()
                self.sent.append(copy)
        prepare(4)

    def result(self, part):
        total = self.own[0, :, part * WIDE : (part + 1) * WIDE]
        for way in range(2):
            self.hop(way, 3, part).wait_recv()
            total = total + self.came[way, 3, part].astype(F32)
        return total

    def drain(self):
        for copy in self.sent:
            copy.wait_send()


def turns():
    some = PARTS // 2
    return [
        (turn, way, (way if turn == 0 else 1 - way) * some + i)
        for turn in range(2)
        for i in range(some)
        for way in range(2)
    ]


def kernel(*refs):
    inputs, o_ref, scratch = refs[:15], refs[15], refs[16:]
    held, scratch = scratch[:15], scratch[15:]
    (own, out, came, res, tokens, normed, table, mix, mix_in, xs, ys) = scratch[:11]
    (wsem, csem, msem, tsem, rsem, gsem, *seq_sems) = scratch[11:]
    (hid_ref, q, k, v, g, ld, wr, gain, ow, post_ref, ids_ref, route_ref, gw, uw, dw) = held
    weights = (8, 12, 13, 14)

    place = lax.axis_index("exp")
    z, core = lax.div(place, 2), lax.rem(place, 2)
    chips = [lax.rem(z + d, 8) * 2 + core for d in range(8)]
    sibling = z * 2 + (1 - core)
    ring = (chips[1], chips[7])
    turn_at = lax.axis_index("seq")
    x, y = lax.rem(turn_at, 4), lax.div(turn_at, 4)
    x_peers = [y * 4 + lax.rem(x + d, 4) for d in range(4)]
    y_peers = [lax.rem(y + d, 4) * 4 + x for d in range(4)]
    at = (x, y, x_peers, y_peers)
    ys[...] = jnp.zeros_like(ys)
    meet = greet(
        [("seq", peer) for peer in x_peers[1:] + y_peers[1:]]
        + [("exp", peer) for peer in chips[1:] + [sibling]]
    )

    loads, shared = [], []
    for i, (src, dst) in enumerate(zip(inputs, held)):
        if i in weights:
            flat = src if i == 8 else src.at[0]
            n = weights.index(i)
            shared.append(
                send_to(flat, dst.at[core], csem.at[0, n], csem.at[1, n], "exp", sibling)
            )
            dst, src = dst.at[core], flat
        loads.append(pltpu.make_async_copy(src, dst, wsem.at[i]))
    arriving = [
        send_to(
            held[i].at[1 - core], held[i].at[1 - core], csem.at[0, n], csem.at[1, n], "exp", sibling
        )
        for n, i in enumerate(weights)
    ]
    early, middle = (2, 5, 6, 3, 1), (10, 11, 4, 7, 0, 9)
    for i in early + middle:
        loads[i].start()

    def need(*which):
        for i in which:
            loads[i].wait()

    lane = lax.broadcasted_iota(jnp.int32, (32, 128), 1).astype(F32)
    sent = []

    def begin(copy):
        copy.start()
        sent.append(copy)

    def give():
        for i, copy in zip(weights, shared):
            loads[i].start()
            copy.start()

    def late():
        for i in middle:
            loads[i].wait()
        ids = ids_ref[...].astype(F32)
        routes = route_ref[...].astype(F32)
        same = lax.broadcasted_iota(jnp.int32, (32, 32), 0) == lax.broadcasted_iota(
            jnp.int32, (32, 32), 1
        )
        shares = jnp.zeros((32, 128), F32)
        for j in range(4):
            named, share = (
                jnp.sum(jnp.where(same, a[j : j + 1, :], 0.0), axis=1, keepdims=True)
                for a in (ids, routes)
            )
            shares = shares + jnp.where(lane == named, share, 0.0)
        table[0] = shares.astype(BF16)
        for d in range(1, 8):
            begin(share_table(d))

    def share_table(d):
        return send_to(
            table.at[0], table.at[8 - d], tsem.at[0, 8 - d], tsem.at[1, 8 - d], "exp", chips[d]
        )

    def mix_copy(h):
        return send_to(
            mix.at[1 - core, h], mix_in.at[h], msem.at[0, h], msem.at[1, h], "exp", sibling
        )

    drain_seq = seq_part(
        q,
        k,
        v,
        g,
        ld,
        wr,
        gain,
        mix,
        xs,
        ys,
        seq_sems,
        at,
        need,
        meet,
        give,
        late,
        lambda h: begin(mix_copy(h)),
    )

    def mixed_rows(ref, offsets):
        rows = [pl.ds(pl.multiple_of(lax.rem(z + d, 8) * 32, 32), 32) for d in offsets]
        return jnp.concatenate(
            [jnp.concatenate([ref[h, r] for h in range(2)], axis=1) for r in rows], axis=0
        )

    def project(offsets):
        block = mm(mixed_rows(mix_in, offsets), ow[1 - core])
        for i, d in enumerate(offsets):
            own[0, d] = own[0, d] + block[32 * i : 32 * i + 32]

    loads[8].wait()
    block = mm(mixed_rows(mix.at[core], range(8)), ow[core])
    for d in range(8):
        own[0, d] = block[32 * d : 32 * d + 32]
    arriving[0].wait_recv()
    for h in range(2):
        mix_copy(h).wait_recv()
    first = RingSum(own.at[0], out.at[0], came.at[0], rsem.at[0], ring)
    project((4,))
    for turn, way, part in turns():
        if turn == 0:
            first.launch(way, part)
    first.run(lambda step: project(((4,), (3, 5), (2, 6), (1, 7), (0,))[step]))
    def onward(way, step, part):
        src = (8 - step) % 8 if way == 0 else step
        dst = 7 - step if way == 0 else step + 1
        return send_to(
            tokens.at[src, part],
            tokens.at[dst, part],
            gsem.at[0, way, step, part],
            gsem.at[1, way, step, part],
            "exp",
            ring[way],
        )

    def settle(offsets):
        for d in offsets:
            row = jnp.concatenate([tokens[d, part] for part in range(PARTS)], axis=1).astype(F32)
            scale = lax.rsqrt(jnp.mean(row * row, axis=-1, keepdims=True) + EPS)
            normed[d] = (row * scale * post_ref[...]).astype(BF16)

    def expert(offsets):
        for d in offsets:
            if d > 0:
                share_table(8 - d).wait_recv()
        shares = jnp.concatenate([table[d] for d in offsets], axis=0).astype(F32)
        lanes = lax.broadcasted_iota(jnp.int32, shares.shape, 1)
        hidden, share = [], []

        def close(e, gate, up):
            hidden.append((gate / (1.0 + jnp.exp(-gate)) * up).astype(BF16))
            share.append(
                jnp.sum(jnp.where(lanes == z * 2 + e, shares, 0.0), axis=1, keepdims=True)
            )

        def widen(e):
            picked = jnp.concatenate([normed[d] for d in offsets], axis=0)
            close(e, mm(picked, gw[e]), mm(picked, uw[e]))

        def widen_late():
            sums = [[0.0, 0.0], [0.0, 0.0]]
            square = 0.0
            for i in range(PARTS // 2):
                for way in range(2):
                    onward(way, 3, way * (PARTS // 2) + i).wait_recv()
                for part in (i, PARTS // 2 + i):
                    cols = slice(part * WIDE, (part + 1) * WIDE)
                    row = jnp.concatenate([tokens[d, part] for d in offsets], axis=0).astype(F32)
                    square = square + jnp.sum(row * row, axis=-1, keepdims=True)
                    row = (row * post_ref[:, cols]).astype(BF16)
                    for e in range(2):
                        for k, w in enumerate((gw, uw)):
                            sums[e][k] = sums[e][k] + mm(row, w[e, cols, :])
            scale = lax.rsqrt(square * (1.0 / D) + EPS)
            for e in range(2):
                close(e, sums[e][0] * scale, sums[e][1] * scale)

        def down(part):
            cols = slice(part * WIDE, (part + 1) * WIDE)
            total = sum(
                mm(hidden[e], dw[e, :, cols]).astype(BF16).astype(F32) * share[e]
                for e in range(2)
            )
            for i, d in enumerate(offsets):
                own[1, d, :, cols] = total[32 * i : 32 * i + 32]

        return widen, widen_late, down

    for part in (i + j for i in range(PARTS // 2) for j in (0, PARTS // 2)):
        cols = slice(part * WIDE, (part + 1) * WIDE)
        block = hid_ref[:, cols].astype(F32) + first.result(part)
        res[:, cols] = block
        tokens[0, part] = block.astype(BF16)
        ahead = 0 if part < PARTS // 2 else 1
        for way in (ahead, 1 - ahead):
            begin(onward(way, 0, part))
    settle((0,))
    for i in weights[1:]:
        loads[i].wait()
    for copy in arriving[1:]:
        copy.wait_recv()

    def pass_on(step):
        for turn, way, part in turns():
            onward(way, step - 1, part).wait_recv()
            if step < 3 or turn == 0:
                begin(onward(way, step, part))
        if step < 3:
            settle((8 - step, step))

    pass_on(1)
    near_widen, _, near_down = expert((0, 1, 7))
    near_widen(0)
    near_widen(1)
    pass_on(2)
    for part in range(PARTS):
        near_down(part)
    next_widen, _, next_down = expert((2, 6))
    next_widen(0)
    pass_on(3)
    next_widen(1)
    for part in range(PARTS):
        next_down(part)
    second = RingSum(own.at[1], out.at[1], came.at[1], rsem.at[1], ring)
    _, widen_late, down = expert((3, 4, 5))
    widen_late()
    for turn, way, part in turns():
        if turn == 0:
            down(part)
            second.launch(way, part)
    second.run(lambda step: None)
    for part in (i + j for i in range(PARTS // 2) for j in (0, PARTS // 2)):
        cols = slice(part * WIDE, (part + 1) * WIDE)
        o_ref[:, cols] = (res[:, cols] + second.result(part)).astype(BF16)
    for copy in sent + shared:
        copy.wait_send()
    first.drain()
    second.drain()
    drain_seq()


def per_device(*args):
    args = list(args)
    args[7] = args[7].reshape(1, DV)
    args[9] = args[9].reshape(1, D)
    args[10] = args[10].T
    args[11] = args[11].T
    slots = pltpu.VMEM((4, 2, DK, 2 * DK), BF16)
    both = {8: (2,) + args[8].shape}
    for i in (12, 13, 14):
        both[i] = (2,) + args[i].shape[1:]
    scratch = [pltpu.VMEM(both.get(i, a.shape), a.dtype) for i, a in enumerate(args)] + [
        pltpu.VMEM((2, 8, 32, D), F32),
        pltpu.VMEM((2, 2, 4, PARTS, 32, WIDE), BF16),
        pltpu.VMEM((2, 2, 4, PARTS, 32, WIDE), BF16),
        pltpu.VMEM((32, D), F32),
        pltpu.VMEM((8, PARTS, 32, WIDE), BF16),
        pltpu.VMEM((8, 32, D), BF16),
        pltpu.VMEM((8, 32, 128), BF16),
        pltpu.VMEM((2, 2, 256, DV), BF16),
        pltpu.VMEM((2, 256, DV), BF16),
        slots,
        slots,
        pltpu.SemaphoreType.DMA((15,)),
        pltpu.SemaphoreType.DMA((2, 4)),
        pltpu.SemaphoreType.DMA((2, 2)),
        pltpu.SemaphoreType.DMA((2, 8)),
        pltpu.SemaphoreType.DMA((2, 2, 2, 4, PARTS)),
        pltpu.SemaphoreType.DMA((2, 2, 4, PARTS)),
    ]
    return pl.pallas_call(
        kernel,
        out_shape=jax.ShapeDtypeStruct(args[0].shape, BF16),
        in_specs=[pl.BlockSpec(memory_space=pl.ANY)] * 15,
        out_specs=pl.BlockSpec(memory_space=pltpu.VMEM),
        scratch_shapes=scratch + [pltpu.SemaphoreType.DMA((4, 4))] * 4,
        compiler_params=pltpu.CompilerParams(
            collective_id=0, has_side_effects=True, vmem_limit_bytes=62 * 1024 * 1024
        ),
        name="layer",
    )(*args)


def solution(mesh):
    in_specs = (
        P(("seq", "exp"), None),
        P("seq", "exp"),
        P("seq", "exp"),
        P("seq", "exp"),
        P("seq", "exp"),
        P("exp", "seq"),
        P("exp", "seq"),
        P(),
        P("exp", None),
        P(),
        P(("seq", "exp"), None),
        P(("seq", "exp"), None),
        P("exp", None, None),
        P("exp", None, None),
        P("exp", None, None),
    )
    out_specs = P(("seq", "exp"), None)
    return jax.shard_map(
        per_device, mesh=mesh, in_specs=in_specs, out_specs=out_specs, check_vma=False
    )
```
